32 devices in a mesh: seq: 2 (over core), ctx: 4 (over z), fsdp: 4 (over y, x).
Axes of the slice: x: 2, y: 2, z: 4, core: 2. Of those that a mesh axis runs over, the one named last changes fastest.
Arguments:
- inputs: bfloat16 [8, 1024, 640], P(('seq', 'fsdp'), 'ctx'), may hold values from -6 to 6
- positions: int32 [8, 1024], P(('seq', 'fsdp'), 'ctx'), may hold values from 0 to 1023, as said below
- block_ids: int32 [8, 8], P(('seq', 'fsdp'), 'ctx'), may hold values from 0 to 7, as said below
- w_query: bfloat16 [640, 1024], P('fsdp'), may hold values from -0.25 to 0.25
- w_key: bfloat16 [640, 256], P('fsdp'), may hold values from -0.25 to 0.25
- w_value: bfloat16 [640, 256], P('fsdp'), may hold values from -0.25 to 0.25
- w_out: bfloat16 [1024, 640], P('fsdp'), may hold values from -0.1875 to 0.1875
- w_gate: bfloat16 [640, 2048], P(None, 'fsdp'), may hold values from -0.25 to 0.25
- w_up: bfloat16 [640, 2048], P(None, 'fsdp'), may hold values from -0.25 to 0.25
- w_down: bfloat16 [2048, 640], P('fsdp'), may hold values from -0.125 to 0.125
- gain_in: bfloat16 [640], P('fsdp'), may hold values from 0.25 to 1.75
- gain_query: bfloat16 [256], P('fsdp'), may hold values from 0.25 to 1.75
- gain_key: bfloat16 [256], P('fsdp'), may hold values from 0.25 to 1.75
- gain_attn: bfloat16 [640], P('fsdp'), may hold values from 0.25 to 1.75
- gain_pre: bfloat16 [640], P('fsdp'), may hold values from 0.25 to 1.75
- gain_post: bfloat16 [640], P('fsdp'), may hold values from 0.25 to 1.75
- cotangent: bfloat16 [8, 1024, 640], P(('seq', 'fsdp'), 'ctx'), may hold values from -6 to 6
Outputs:
- result: float32 [8, 1024, 640], P(('seq', 'fsdp'), 'ctx')
- input_grad: float32 [8, 1024, 640], P(('seq', 'fsdp'), 'ctx')
- grad_w_query: float32 [640, 1024], P('fsdp')
- grad_w_key: float32 [640, 256], P('fsdp')
- grad_w_value: float32 [640, 256], P('fsdp')
- grad_w_out: float32 [1024, 640], P('fsdp')
- grad_w_gate: float32 [640, 2048], P(None, 'fsdp')
- grad_w_up: float32 [640, 2048], P(None, 'fsdp')
- grad_w_down: float32 [2048, 640], P('fsdp')
- grad_gain_in: float32 [640], P('fsdp')
- grad_gain_query: float32 [256], P('fsdp')
- grad_gain_key: float32 [256], P('fsdp')
- grad_gain_attn: float32 [640], P('fsdp')
- grad_gain_pre: float32 [640], P('fsdp')
- grad_gain_post: float32 [640], P('fsdp')
The draws below stay inside these ranges and needn't reach their ends.
Inputs may be any that keep to these rules, and one draw needn't show every extreme that they name: `block_ids`: in every sequence the entries at 2 c and 2 c + 1 are b and 7 - b with b below 4, so a sequence's entries are a permutation of its blocks. `positions`: A token's position counts the tokens before it in its document, documents following one another in the order given by order; every document has at most 1024 tokens and the first of each sequence exactly 1024.
All inputs are finite; a program needn't handle non-finite values.
Results may differ from the reference program's by a relative error of at most 0.022.
Values may be sent and summed in bfloat16 or wider, within the bound.
No kernel may reach another device: no remote copies, remote signals or barrier semaphores. Data moves between devices by JAX's collectives and lax.ppermute only.
A program may use at most 192 MiB of HBM per device.

```python
import jax
import jax.numpy as jnp
from jax import lax

D = 640
HEADS = 4
HEAD_DIM = 256
FF = 2048
LEN = 1024
SLOTS = 8
BLK = 128
SEQS = 8
DOC_MOST = 1024


def pair_layout(key):
    half_slots = SLOTS // 2
    seq_keys = jax.random.split(jax.random.fold_in(key, 11), SEQS)
    picked = jax.vmap(lambda one_key: jax.random.permutation(one_key, half_slots))(seq_keys).astype(jnp.int32)
    return jnp.stack([picked, SLOTS - 1 - picked], axis=-1).reshape(SEQS, SLOTS).astype(jnp.int32)


def draw_block_ids(key, part):
    return pair_layout(key)


def draw_positions(key, part):
    blocks = pair_layout(key)
    index = jnp.arange(LEN, dtype=jnp.int32)
    starts_drawn = jax.random.randint(jax.random.fold_in(key, 12), (SEQS, LEN), 0, 384) == 0
    flags = starts_drawn & (index >= DOC_MOST)[None, :] | (index % DOC_MOST == 0)[None, :]
    starts = lax.cummax(jnp.where(flags, index[None, :], 0), axis=1)
    local_pos = index[None, :] - starts
    order = (blocks[:, :, None] * BLK + jnp.arange(BLK, dtype=jnp.int32)[None, None, :]).reshape(SEQS, LEN)
    return jnp.take_along_axis(local_pos, order, axis=1).astype(jnp.int32)


def levels(key, dims, cuts, low, top_value):
    def one(position, parts):
        steps = jax.random.uniform(jax.random.fold_in(jax.random.fold_in(key, 6), position), (parts,), jnp.float32, low / len(cuts), top_value / len(cuts))
        return jnp.repeat(jnp.exp(steps), dims[position] // parts).reshape((-1,) + (1,) * (len(dims) - position - 1))

    factor_of = one(*cuts[0])
    for cut in cuts[1:]:
        factor_of = factor_of * one(*cut)
    return factor_of


def gaussian(key, shape, deviation, bound, shards=(), kind=jnp.bfloat16):
    level = levels(key, shape, shards, -0.22, 0.18) if shards else 1.0
    result = jax.random.normal(key, shape, jnp.float32) * deviation * level
    return jnp.minimum(jnp.maximum(result, -bound), bound).astype(kind)


def setup_inputs(seed: int = 0) -> dict:
    seeds = jax.random.split(jax.random.key(seed), 18)
    inputs = gaussian(seeds[0], (SEQS, LEN, D), 1.0, 6.0, ((0, 8), (1, 4)))
    positions = draw_positions(jax.random.fold_in(seeds[17], 71), 0)
    block_ids = draw_block_ids(jax.random.fold_in(seeds[17], 71), 0)
    w_query = gaussian(seeds[3], (D, HEADS * HEAD_DIM), D ** -0.5, 0.25, ((0, 4),))
    w_key = gaussian(seeds[4], (D, HEAD_DIM), D ** -0.5, 0.25, ((0, 4),))
    w_value = gaussian(seeds[5], (D, HEAD_DIM), D ** -0.5, 0.25, ((0, 4),))
    w_out = gaussian(seeds[6], (HEADS * HEAD_DIM, D), (HEADS * HEAD_DIM) ** -0.5, 0.1875, ((0, 4),))
    w_gate = gaussian(seeds[7], (D, FF), D ** -0.5, 0.25, ((1, 4),))
    w_up = gaussian(seeds[8], (D, FF), D ** -0.5, 0.25, ((1, 4),))
    w_down = gaussian(seeds[9], (FF, D), FF ** -0.5, 0.125, ((0, 4),))
    gain_in = jnp.clip(1.0 + 0.15 * jax.random.normal(seeds[10], (D,), jnp.float32), 0.25, 1.75).astype(jnp.bfloat16)
    gain_query = jnp.clip(1.0 + 0.15 * jax.random.normal(seeds[11], (HEAD_DIM,), jnp.float32), 0.25, 1.75).astype(jnp.bfloat16)
    gain_key = jnp.clip(1.0 + 0.15 * jax.random.normal(seeds[12], (HEAD_DIM,), jnp.float32), 0.25, 1.75).astype(jnp.bfloat16)
    gain_attn = jnp.clip(1.0 + 0.15 * jax.random.normal(seeds[13], (D,), jnp.float32), 0.25, 1.75).astype(jnp.bfloat16)
    gain_pre = jnp.clip(1.0 + 0.15 * jax.random.normal(seeds[14], (D,), jnp.float32), 0.25, 1.75).astype(jnp.bfloat16)
    gain_post = jnp.clip(1.0 + 0.15 * jax.random.normal(seeds[15], (D,), jnp.float32), 0.25, 1.75).astype(jnp.bfloat16)
    cotangent = gaussian(seeds[16], (SEQS, LEN, D), 1.0, 6.0, ((0, 8), (1, 4)))
    return dict(inputs=inputs, positions=positions, block_ids=block_ids, w_query=w_query, w_key=w_key, w_value=w_value, w_out=w_out, w_gate=w_gate, w_up=w_up, w_down=w_down, gain_in=gain_in, gain_query=gain_query, gain_key=gain_key, gain_attn=gain_attn, gain_pre=gain_pre, gain_post=gain_post, cotangent=cotangent)


EPS = 1e-06
THETA = 1000000.0
NEG = -1e+30

@jax.custom_vjp
def low(v):
    return lax.optimization_barrier(v.astype(jnp.bfloat16)).astype(jnp.float32)

@jax.custom_vjp
def low_back(v):
    return v

def low_keep(v):
    return (low(v), None)

def low_pass(kept, grad):
    return (grad,)

def back_keep(v):
    return (v, None)

def back_low(kept, grad):
    return (low(grad),)
low.defvjp(low_keep, low_pass)
low_back.defvjp(back_keep, back_low)

def dense(left, right):
    return jnp.dot(left, right, precision=lax.Precision.HIGHEST)

def rmsnorm(value, gain):
    return value * lax.rsqrt(lax.optimization_barrier(jnp.mean(value * value, axis=-1, keepdims=True)) + EPS) * gain

def rotate(value, cosine, sine_table):
    half = value.shape[-1] // 2
    first = value[..., :half]
    second = value[..., half:]
    return jnp.concatenate([first * cosine - second * sine_table, second * cosine + first * sine_table], axis=-1)

def tables(positions, head_size):
    half = head_size // 2
    freq = 1.0 / THETA ** (jnp.arange(half, dtype=jnp.float32) * 2.0 / head_size)
    angle = positions.astype(jnp.float32)[:, None] * freq[None, :]
    return (jnp.cos(angle), jnp.sin(angle))

def gelu_tanh(value):
    return jax.nn.gelu(value, approximate=True)

def layer(inputs, params, order, cosine, sine_table):
    w_query, w_key, w_value, w_out, w_gate, w_up, w_down, gain_in, gain_query, gain_key, gain_attn, gain_pre, gain_post = params
    length = inputs.shape[0]
    head_size = gain_query.shape[0]
    head_count = w_query.shape[1] // head_size
    hidden_in = low(rmsnorm(inputs, gain_in))
    query_pre = low_back(dense(hidden_in, w_query)).reshape(length, head_count, head_size)
    key_pre = low_back(dense(hidden_in, w_key))
    values = low(low_back(dense(hidden_in, w_value)))
    queries = low(rotate(rmsnorm(query_pre, gain_query), cosine[:, None], sine_table[:, None]))
    key_rows = low(rotate(rmsnorm(key_pre, gain_key), cosine, sine_table))
    block_rows = min(512, length)
    score_scale = head_size ** (-0.5)

    def attend(item):
        query_block, order_block = item
        scores = low_back(jnp.einsum('qhd,kd->hqk', query_block, key_rows, precision=lax.Precision.HIGHEST) * score_scale)
        allowed = order[None, None, :] <= order_block[None, :, None]
        scores = jnp.where(allowed, scores, NEG)
        highest = lax.optimization_barrier(jnp.max(scores, axis=-1, keepdims=True))
        weights = jnp.exp(scores - highest)
        probs = weights / lax.optimization_barrier(jnp.sum(weights, axis=-1, keepdims=True))
        return jnp.einsum('hqk,kd->qhd', low(probs), values, precision=lax.Precision.HIGHEST)
    context = lax.map(jax.checkpoint(attend), (queries.reshape(length // block_rows, block_rows, head_count, head_size), order.reshape(length // block_rows, block_rows)))
    context = low(low_back(context.reshape(length, head_count * head_size)))
    attn_out = low_back(dense(context, w_out))
    middle = inputs + rmsnorm(attn_out, gain_attn)
    ffn_in = low(rmsnorm(middle, gain_pre))
    gate_pre = low_back(dense(ffn_in, w_gate))
    up_pre = low_back(dense(ffn_in, w_up))
    mixed = low(gelu_tanh(gate_pre) * up_pre)
    ffn_out = low_back(dense(mixed, w_down))
    return middle + rmsnorm(ffn_out, gain_post)

def reference(inputs, positions, block_ids, w_query, w_key, w_value, w_out, w_gate, w_up, w_down, gain_in, gain_query, gain_key, gain_attn, gain_pre, gain_post, cotangent):
    params = tuple((member.astype(jnp.float32) for member in (w_query, w_key, w_value, w_out, w_gate, w_up, w_down, gain_in, gain_query, gain_key, gain_attn, gain_pre, gain_post)))
    offsets = jnp.arange(BLK, dtype=jnp.int32)

    def one_sequence(totals, item):
        seq_inputs, seq_positions, seq_blocks, seq_cot = item
        order = (seq_blocks.astype(jnp.int32)[:, None] * BLK + offsets[None, :]).reshape(LEN).astype(jnp.int32)
        cosine, sine_table = tables(seq_positions, HEAD_DIM)

        def forward(values_in, weights):
            return layer(values_in, weights, order, cosine, sine_table)
        seq_result, pull = jax.vjp(forward, seq_inputs.astype(jnp.float32), params)
        seq_grad, weight_grads = pull(seq_cot.astype(jnp.float32))
        totals = tuple((before + update for before, update in zip(totals, weight_grads)))
        return (totals, (seq_result, seq_grad))
    zeros = tuple((jnp.zeros(member.shape, jnp.float32) for member in params))
    totals, (results, input_grads) = lax.scan(one_sequence, zeros, (inputs, positions, block_ids, cotangent))
    return (results, input_grads, totals[0], totals[1], totals[2], totals[3], totals[4], totals[5], totals[6], totals[7], totals[8], totals[9], totals[10], totals[11], totals[12])
```

```python
import jax
import jax.numpy as jnp
from jax import lax
from jax.sharding import PartitionSpec as P

EPS = 1e-06
THETA = 1000000.0
NEG = -1e30
BF = jnp.bfloat16
F32 = jnp.float32


def matmul(left, right):
    return jnp.dot(left, right, preferred_element_type=F32)


def inner_cols(left, right):
    return lax.dot_general(left, right, (((1,), (1,)), ((), ())), preferred_element_type=F32)


def inner_rows(left, right):
    return lax.dot_general(left, right, (((0,), (0,)), ((), ())), preferred_element_type=F32)


def norm_fwd(value, gain):
    inverse = lax.rsqrt(jnp.mean(value * value, axis=-1, keepdims=True) + EPS)
    return (value * inverse * gain, inverse)


def norm_back(value, inverse, gain, grad):
    scaled = value * inverse
    gain_grad = jnp.sum((grad * scaled).reshape(-1, value.shape[-1]), axis=0)
    weighted = grad * gain
    value_grad = inverse * (weighted - scaled * jnp.mean(weighted * scaled, axis=-1, keepdims=True))
    return (value_grad, gain_grad)


def rotate(value, cosine, sine_table):
    half = value.shape[-1] // 2
    first = value[..., :half]
    second = value[..., half:]
    return jnp.concatenate(
        [first * cosine - second * sine_table, second * cosine + first * sine_table], axis=-1
    )


def tables(positions, head_size):
    half = head_size // 2
    freq = 1.0 / THETA ** (jnp.arange(half, dtype=F32) * 2.0 / head_size)
    angle = positions.astype(F32)[:, None] * freq[None, :]
    return (jnp.cos(angle), jnp.sin(angle))


def gelu_tanh(value):
    return jax.nn.gelu(value, approximate=True)


def swap(value, axis, flip, size):
    return lax.ppermute(value, axis, [(i, i ^ flip) for i in range(size)])


def swap_pair(value):
    return swap(value, "seq", 1, 2)


def swap_split(value, axis, size, flip0, flip1):
    perm = [(i, i ^ flip0) for i in range(size)]
    perm += [(size + i, size + (i ^ flip1)) for i in range(size)]
    return lax.ppermute(value, ("seq", axis), perm)


def gather4(value, core, axis, size, first, second):
    one = swap(value, axis, first, size)
    two = swap(value, axis, second, size)
    both = swap_split(jnp.where(core == 0, one, two), axis, size, second, first)
    return [value, one, two, both]


def scatter4(blocks, core, axis, size, first, second):
    via = swap_split(blocks[3], axis, size, second, first).astype(F32)
    none = jnp.zeros_like(via)
    one = (blocks[1].astype(F32) + jnp.where(core == 0, via, none)).astype(BF)
    two = (blocks[2].astype(F32) + jnp.where(core == 0, none, via)).astype(BF)
    one = swap(one, axis, first, size).astype(F32)
    two = swap(two, axis, second, size).astype(F32)
    return blocks[0].astype(F32) + one + two


def halves(value, pick):
    rows = value.shape[0] // 2
    keep = lax.dynamic_slice_in_dim(value, pick * rows, rows, 0)
    send = lax.dynamic_slice_in_dim(value, (1 - pick) * rows, rows, 0)
    return keep, send


def join(mine, other, pick):
    return jnp.where(
        pick == 0, jnp.concatenate([mine, other], 0), jnp.concatenate([other, mine], 0)
    )


def ctx_sum(value, size, order):
    if size != 4:
        return lax.psum(value.astype(BF), "ctx")
    place = lax.axis_index("ctx")
    high = place // 2
    odd = lax.rem(place, 2)
    mixed = lax.rem(high + odd, 2)
    steps = [(1, mixed), (3, high)] if order == 0 else [(3, high), (1, mixed)]
    for flip, pick in steps:
        keep, send = halves(value, pick)
        value = keep.astype(F32) + swap(send.astype(BF), "ctx", flip, 4).astype(F32)
    value = value.astype(BF)
    for flip, pick in steps[::-1]:
        value = join(value, swap(value, "ctx", flip, 4), pick)
    return value


def attend_forward(queries, key_rows, values, query_order, key_order, score_scale):
    allowed = key_order[None, :] <= query_order[:, None]
    outputs = []
    logsums = []
    for head_index in range(queries.shape[1]):
        scores = inner_cols(queries[:, head_index], key_rows) * score_scale
        scores = jnp.where(allowed, scores, NEG)
        highest = jnp.max(scores, axis=-1, keepdims=True)
        weights = jnp.exp(scores - highest)
        summed = jnp.sum(weights, axis=-1, keepdims=True)
        probs = (weights / summed).astype(BF)
        outputs.append(matmul(probs, values))
        logsums.append(highest + jnp.log(summed))
    return (jnp.stack(outputs, axis=1), jnp.stack(logsums, axis=1))


def attend_backward(
    queries, key_rows, values, query_order, key_order, score_scale, logsums, out_grad
):
    allowed = key_order[None, :] <= query_order[:, None]
    query_grads = []
    key_grad = jnp.zeros(key_rows.shape, F32)
    value_grad = jnp.zeros(values.shape, F32)
    for head_index in range(queries.shape[1]):
        query_head = queries[:, head_index]
        grad_head = out_grad[:, head_index]
        scores = inner_cols(query_head, key_rows) * score_scale
        scores = jnp.where(allowed, scores, NEG)
        probs = jnp.exp(scores - logsums[:, head_index])
        value_grad = value_grad + inner_rows(probs.astype(BF), grad_head)
        prob_grad = inner_cols(grad_head, values)
        weighted = jnp.sum(probs * prob_grad, axis=-1, keepdims=True)
        score_grad = (probs * (prob_grad - weighted)).astype(BF)
        query_grads.append(matmul(score_grad, key_rows) * score_scale)
        key_grad = key_grad + inner_rows(score_grad, query_head) * score_scale
    return (jnp.stack(query_grads, axis=1), key_grad, value_grad)


def place_rows(blocks, fsdp):
    rows = blocks[0].shape[0]
    whole = jnp.zeros((4 * rows, blocks[0].shape[1]), blocks[0].dtype)
    for flip, block in enumerate(blocks):
        whole = lax.dynamic_update_slice_in_dim(whole, block, (fsdp ^ flip) * rows, 0)
    return whole


def pick_half(value, which, axis):
    size = value.shape[axis] // 2
    return lax.dynamic_slice_in_dim(value, which * size, size, axis)


def on_device(ctx_size):
    def run(
        inputs,
        positions,
        block_ids,
        w_query,
        w_key,
        w_value,
        w_out,
        w_gate,
        w_up,
        w_down,
        gain_in,
        gain_query,
        gain_key,
        gain_attn,
        gain_pre,
        gain_post,
        cotangent,
    ):
        core = lax.axis_index("seq")
        fsdp = lax.axis_index("fsdp")
        seq_rows, model_width = inputs.shape[1:]
        head_size = gain_query.shape[0] * 4
        head_count = w_query.shape[1] // head_size
        half_rows = seq_rows // 2
        score_scale = head_size ** (-0.5)

        gains = [gain_in, gain_attn, gain_pre, gain_post, gain_query, gain_key]
        gain_sizes = [member.shape[0] for member in gains]
        gain_row = jnp.concatenate(gains)
        kv_width = 2 * head_size
        gain_rows = -(-gain_row.shape[0] // kv_width)
        gain_row = jnp.pad(gain_row, (0, gain_rows * kv_width - gain_row.shape[0]))
        packed = jnp.concatenate(
            [jnp.concatenate([w_key, w_value], 1), gain_row.reshape(gain_rows, kv_width)], 0
        )
        shard_rows = w_key.shape[0]
        packed = lax.all_gather(packed, "fsdp", axis=0)
        kv_full = packed[:, :shard_rows].reshape(4 * shard_rows, kv_width)
        gain_full = packed[:, shard_rows:].reshape(4, -1).astype(F32)
        norms = []
        start = 0
        for size in gain_sizes:
            norms.append(gain_full[:, start : start + size].reshape(-1))
            start += size
        norm_in, norm_attn, norm_pre, norm_post, norm_query, norm_key = norms

        def fetch(shard, axis):
            mine = gather4(pick_half(shard, core, axis), core, "fsdp", 4, 1, 2)
            other = [pick_half(shard, 1 - core, axis)]
            other += [swap_pair(block) for block in mine[1:]]
            return mine, other

        def whole_rows(pair):
            mine, other = pair
            low = [jnp.where(core == 0, a, b) for a, b in zip(mine, other)]
            high = [jnp.where(core == 0, b, a) for a, b in zip(mine, other)]
            return place_rows([jnp.concatenate([a, b], 0) for a, b in zip(low, high)], fsdp)

        query_full = whole_rows(fetch(w_query, 0))
        out_full = whole_rows(fetch(w_out, 0))
        gate_up = jnp.concatenate(
            [pick_half(w_gate, core, 1), pick_half(w_up, core, 1)], 1
        )
        gate_up_other = jnp.concatenate(
            [pick_half(w_gate, 1 - core, 1), pick_half(w_up, 1 - core, 1)], 1
        )
        gu_mine = gather4(gate_up, core, "fsdp", 4, 1, 2)
        gu_all = gu_mine + [gate_up_other] + [swap_pair(block) for block in gu_mine[1:]]
        down_mine, down_other = fetch(w_down, 0)
        unit = gate_up.shape[1] // 2
        gate_full = jnp.concatenate([block[:, :unit] for block in gu_all], 1)
        up_full = jnp.concatenate([block[:, unit:] for block in gu_all], 1)
        down_full = jnp.concatenate(down_mine + down_other, 0)

        offsets = jnp.arange(half_rows, dtype=jnp.int32)
        blocks = block_ids[0]
        query_order = (blocks[:, None] * half_rows + offsets[None, :]).reshape(seq_rows)
        cosine, sine_table = tables(positions[0], head_size)
        residual = inputs[0].astype(F32)
        normed_in, inverse_in = norm_fwd(residual, norm_in)
        hidden_in = normed_in.astype(BF)
        kv_pre = matmul(hidden_in, kv_full)
        key_pre = kv_pre[:, :head_size]
        key_normed, inverse_key = norm_fwd(key_pre, norm_key)
        key_rows = rotate(key_normed, cosine, sine_table).astype(BF)
        ids_row = jnp.broadcast_to(blocks.astype(BF)[:, None], (2, kv_width))
        packed_kv = jnp.concatenate(
            [
                jnp.concatenate([key_rows, kv_pre[:, head_size:].astype(BF)], 1),
                jnp.pad(ids_row, ((0, 14), (0, 0))),
            ],
            0,
        )
        if ctx_size == 4:
            kv_blocks = gather4(packed_kv, core, "ctx", 4, 1, 3)
            kv_all = jnp.stack(kv_blocks, 0)
        else:
            kv_all = lax.all_gather(packed_kv, "ctx", axis=0)
        block_all = kv_all[:, seq_rows : seq_rows + 2, 0].astype(jnp.int32)
        key_order = (block_all[:, :, None] * half_rows + offsets[None, None, :]).reshape(-1)
        key_all = kv_all[:, :seq_rows, :head_size].reshape(-1, head_size)
        value_all = kv_all[:, :seq_rows, head_size:].reshape(-1, head_size)

        query_pre = matmul(hidden_in, query_full).reshape(seq_rows, head_count, head_size)
        query_normed, inverse_query = norm_fwd(query_pre, norm_query)
        queries = rotate(query_normed, cosine[:, None], sine_table[:, None]).astype(BF)
        seq_out, logsum = attend_forward(
            queries, key_all, value_all, query_order, key_order, score_scale
        )
        context = seq_out.astype(BF).reshape(seq_rows, head_count * head_size)
        attn_out = matmul(context, out_full)
        attn_normed, inverse_attn = norm_fwd(attn_out, norm_attn)
        middle = residual + attn_normed
        pre_normed, inverse_pre = norm_fwd(middle, norm_pre)
        ffn_in = pre_normed.astype(BF)

        gate_pre = matmul(ffn_in, gate_full)
        up_pre = matmul(ffn_in, up_full)
        activated, gelu_pull = jax.vjp(gelu_tanh, gate_pre)
        mixed = (activated * up_pre).astype(BF)
        ffn_out = matmul(mixed, down_full)
        ffn_normed, inverse_post = norm_fwd(ffn_out, norm_post)
        result = middle + ffn_normed
        grad_output = cotangent[0].astype(F32)
        ffn_grad, grad_post = norm_back(ffn_out, inverse_post, norm_post, grad_output)
        ffn_grad = ffn_grad.astype(BF)
        mixed_grad = inner_cols(ffn_grad, down_full)
        gate_grad = gelu_pull(mixed_grad * up_pre)[0].astype(BF)
        up_grad = (mixed_grad * activated).astype(BF)
        pre_grad = inner_cols(gate_grad, gate_full) + inner_cols(up_grad, up_full)

        hidden_half = mixed.shape[1] // 2
        both = lambda value: (value, swap_pair(value))
        split = lambda value: (value[:, :hidden_half], swap_pair(value[:, hidden_half:]))
        in_a, in_b = both(ffn_in)
        fg_a, fg_b = both(ffn_grad)
        mx_a, mx_b = split(mixed)
        gg_a, gg_b = split(gate_grad)
        ug_a, ug_b = split(up_grad)
        d_down = (inner_rows(mx_a, fg_a) + inner_rows(mx_b, fg_b)).astype(BF)
        d_gate = (inner_rows(in_a, gg_a) + inner_rows(in_b, gg_b)).astype(BF)
        d_up = (inner_rows(in_a, ug_a) + inner_rows(in_b, ug_b)).astype(BF)
        cut = lambda value, j: value[:, j * unit : (j + 1) * unit]
        gu_parts = [jnp.concatenate([cut(d_gate, j), cut(d_up, j)], 1) for j in range(4)]
        down_parts = [d_down[j * unit : (j + 1) * unit] for j in range(4)]
        down_sum = ctx_sum(scatter4(down_parts, core, "fsdp", 4, 1, 2), ctx_size, 1)
        gu_sum = ctx_sum(scatter4(gu_parts, core, "fsdp", 4, 1, 2), ctx_size, 0)
        down_other = swap_pair(down_sum)
        gu_other = swap_pair(gu_sum)
        total_down = join(down_sum, down_other, core).astype(F32)
        gate_a, gate_b = gu_sum[:, :unit], gu_other[:, :unit]
        up_a, up_b = gu_sum[:, unit:], gu_other[:, unit:]

        def join_cols(mine, other):
            return jnp.where(
                core == 0,
                jnp.concatenate([mine, other], 1),
                jnp.concatenate([other, mine], 1),
            ).astype(F32)

        total_gate = join_cols(gate_a, gate_b)
        total_up = join_cols(up_a, up_b)

        middle_part, grad_pre = norm_back(middle, inverse_pre, norm_pre, pre_grad)
        middle_grad = grad_output + middle_part
        attn_grad, grad_attn = norm_back(attn_out, inverse_attn, norm_attn, middle_grad)
        attn_grad = attn_grad.astype(BF)
        context_grad = (
            inner_cols(attn_grad, out_full).astype(BF).reshape(seq_rows, head_count, head_size)
        )
        heads = context.reshape(seq_rows, head_count, 2, head_size // 2)
        ctx_mine = lax.dynamic_index_in_dim(heads, core, 2, False).reshape(seq_rows, -1)
        ctx_other = lax.dynamic_index_in_dim(heads, 1 - core, 2, False).reshape(seq_rows, -1)
        d_out = (
            inner_rows(ctx_mine, attn_grad) + inner_rows(swap_pair(ctx_other), swap_pair(attn_grad))
        ).astype(BF)
        out_rows = d_out.shape[0] // 4
        out_parts = [
            lax.dynamic_slice_in_dim(d_out, (fsdp ^ j) * out_rows, out_rows, 0) for j in range(4)
        ]
        out_sum = ctx_sum(scatter4(out_parts, core, "fsdp", 4, 1, 2), ctx_size, 1)
        total_out = join(out_sum, swap_pair(out_sum), core).astype(F32)

        query_back, key_grad, value_grad = attend_backward(
            queries,
            key_all,
            value_all,
            query_order,
            key_order,
            score_scale,
            logsum,
            context_grad,
        )
        kv_grad = jnp.concatenate([key_grad, value_grad], 1).astype(BF)
        if ctx_size == 4:
            kv_parts = [kv_grad[j * seq_rows : (j + 1) * seq_rows] for j in range(4)]
            kv_back = scatter4(kv_parts, core, "ctx", 4, 1, 3)
        else:
            kv_back = lax.psum_scatter(kv_grad, "ctx", scatter_dimension=0, tiled=True).astype(F32)
        query_normed_grad = rotate(query_back, cosine[:, None], -sine_table[:, None])
        query_pre_grad, grad_query = norm_back(
            query_pre, inverse_query, norm_query, query_normed_grad
        )
        query_pre_grad = query_pre_grad.astype(BF).reshape(seq_rows, head_count * head_size)
        value_back = kv_back[:, head_size:].astype(BF)
        key_normed_grad = rotate(kv_back[:, :head_size], cosine, -sine_table)
        key_pre_grad, grad_key = norm_back(key_pre, inverse_key, norm_key, key_normed_grad)
        key_pre_grad = key_pre_grad.astype(BF)
        kv_pre_grad = jnp.concatenate([key_pre_grad, value_back], 1)
        hidden_grad = inner_cols(query_pre_grad, query_full) + inner_cols(kv_pre_grad, kv_full)
        input_part, grad_in = norm_back(residual, inverse_in, norm_in, hidden_grad)
        input_grad = middle_grad + input_part

        wide = jnp.concatenate(
            [query_pre_grad.reshape(seq_rows, 2, -1), kv_pre_grad.reshape(seq_rows, 2, -1)], 2
        )
        mine = lax.dynamic_index_in_dim(wide, core, 1, False)
        other = lax.dynamic_index_in_dim(wide, 1 - core, 1, False)
        d_wide = (
            inner_rows(hidden_in, mine) + inner_rows(swap_pair(hidden_in), swap_pair(other))
        ).astype(BF)
        gain_grads = jnp.concatenate(
            [
                member.reshape(4, -1)
                for member in (grad_in, grad_attn, grad_pre, grad_post, grad_query, grad_key)
            ],
            1,
        ).astype(BF)
        width = d_wide.shape[1]
        gain_rows = -(-gain_grads.shape[1] // width)
        gain_grads = jnp.pad(
            gain_grads, ((0, 0), (0, gain_rows * width - gain_grads.shape[1]))
        ).reshape(4, gain_rows, width)
        gain_grads = jnp.pad(gain_grads, ((0, 0), (0, 32 - gain_rows), (0, 0)))
        late = jnp.concatenate([d_wide.reshape(4, shard_rows, width), gain_grads], 1)
        late_parts = [lax.dynamic_index_in_dim(late, fsdp ^ j, 0, False) for j in range(4)]
        late_sum = ctx_sum(scatter4(late_parts, core, "fsdp", 4, 1, 2), ctx_size, 0)
        late_other = swap_pair(late_sum)
        query_cols = query_pre_grad.shape[1] // 2
        total_query = join_cols(late_sum[:shard_rows, :query_cols], late_other[:shard_rows, :query_cols])
        total_kv = join_cols(late_sum[:shard_rows, query_cols:], late_other[:shard_rows, query_cols:])
        gain_total = late_sum[shard_rows : shard_rows + gain_rows].astype(F32)
        gain_total = gain_total + late_other[shard_rows : shard_rows + gain_rows].astype(F32)
        gain_total = gain_total.reshape(-1)
        outs = []
        start = 0
        for size in gain_sizes:
            outs.append(gain_total[start : start + size])
            start += size
        g_in, g_attn, g_pre, g_post, g_query, g_key = outs
        return (
            result[None],
            input_grad[None],
            total_query,
            total_kv[:, :head_size],
            total_kv[:, head_size:],
            total_out,
            total_gate,
            total_up,
            total_down,
            g_in,
            g_query,
            g_key,
            g_attn,
            g_pre,
            g_post,
        )

    return run


def solution(mesh):
    rows = P(("seq", "fsdp"), "ctx")
    wide = P(("seq", "fsdp"), "ctx", None)
    first = P("fsdp", None)
    second = P(None, "fsdp")
    flat = P("fsdp")
    in_specs = (wide, rows, rows, first, first, first, first, second, second, first)
    in_specs += (flat,) * 6 + (wide,)
    out_specs = (wide, wide, first, first, first, first, second, second, first) + (flat,) * 6
    return jax.shard_map(
        on_device(mesh.shape["ctx"]),
        mesh=mesh,
        in_specs=in_specs,
        out_specs=out_specs,
        check_vma=False,
    )
```

```python
import jax
import jax.numpy as jnp
from jax import lax
from jax.experimental import pallas as pl
from jax.experimental.pallas import tpu as pltpu
from jax.sharding import PartitionSpec as P

EPS = 1e-06
THETA = 1000000.0
NEG = -1e30
BF = jnp.bfloat16
F32 = jnp.float32


def matmul(left, right):
    return jnp.dot(left, right, preferred_element_type=F32)


def inner_cols(left, right):
    return lax.dot_general(left, right, (((1,), (1,)), ((), ())), preferred_element_type=F32)


def inner_rows(left, right):
    return lax.dot_general(left, right, (((0,), (0,)), ((), ())), preferred_element_type=F32)


def rotate(value, cosine, sine_table):
    half = value.shape[-1] // 2
    first = value[..., :half]
    second = value[..., half:]
    return jnp.concatenate(
        [first * cosine - second * sine_table, second * cosine + first * sine_table], axis=-1
    )


def tables(positions, head_size):
    half = head_size // 2
    freq = 1.0 / THETA ** (jnp.arange(half, dtype=F32) * 2.0 / head_size)
    angle = positions.astype(F32)[:, None] * freq[None, :]
    return (jnp.cos(angle), jnp.sin(angle))


def swap(value, axis, flip, size):
    return lax.ppermute(value, axis, [(i, i ^ flip) for i in range(size)])


def swap_pair(value):
    return swap(value, "seq", 1, 2)


def swap_split(value, axis, size, flip0, flip1):
    perm = [(i, i ^ flip0) for i in range(size)]
    perm += [(size + i, size + (i ^ flip1)) for i in range(size)]
    return lax.ppermute(value, ("seq", axis), perm)


def gather4(value, core, axis, size, first, second):
    one = swap(value, axis, first, size)
    two = swap(value, axis, second, size)
    both = swap_split(jnp.where(core == 0, one, two), axis, size, second, first)
    return [value, one, two, both]


def scatter4(blocks, core, axis, size, first, second):
    via = swap_split(blocks[3], axis, size, second, first).astype(F32)
    none = jnp.zeros_like(via)
    one = (blocks[1].astype(F32) + jnp.where(core == 0, via, none)).astype(BF)
    two = (blocks[2].astype(F32) + jnp.where(core == 0, none, via)).astype(BF)
    one = swap(one, axis, first, size).astype(F32)
    two = swap(two, axis, second, size).astype(F32)
    return blocks[0].astype(F32) + one + two


def halves(value, pick):
    rows = value.shape[0] // 2
    keep = lax.dynamic_slice_in_dim(value, pick * rows, rows, 0)
    send = lax.dynamic_slice_in_dim(value, (1 - pick) * rows, rows, 0)
    return keep, send


def join(mine, other, pick):
    return jnp.where(
        pick == 0, jnp.concatenate([mine, other], 0), jnp.concatenate([other, mine], 0)
    )


def ctx_sum(value, size, order):
    if size != 4:
        return lax.psum(value.astype(BF), "ctx")
    place = lax.axis_index("ctx")
    high = place // 2
    odd = lax.rem(place, 2)
    mixed = lax.rem(high + odd, 2)
    steps = [(1, mixed), (3, high)] if order == 0 else [(3, high), (1, mixed)]
    for flip, pick in steps:
        keep, send = halves(value, pick)
        value = keep.astype(F32) + swap(send.astype(BF), "ctx", flip, 4).astype(F32)
    value = value.astype(BF)
    for flip, pick in steps[::-1]:
        value = join(value, swap(value, "ctx", flip, 4), pick)
    return value


def attend_forward(queries, key_rows, values, query_order, key_order, score_scale):
    allowed = key_order[None, :] <= query_order[:, None]
    outputs = []
    logsums = []
    for head_index in range(queries.shape[1]):
        scores = inner_cols(queries[:, head_index], key_rows) * score_scale
        scores = jnp.where(allowed, scores, NEG)
        highest = jnp.max(scores, axis=-1, keepdims=True)
        weights = jnp.exp(scores - highest)
        summed = jnp.sum(weights, axis=-1, keepdims=True)
        probs = (weights / summed).astype(BF)
        outputs.append(matmul(probs, values))
        logsums.append(highest + jnp.log(summed))
    return (jnp.stack(outputs, axis=1), jnp.stack(logsums, axis=1))


def attend_backward(
    queries, key_rows, values, query_order, key_order, score_scale, logsums, out_grad
):
    allowed = key_order[None, :] <= query_order[:, None]
    query_grads = []
    key_grad = jnp.zeros(key_rows.shape, F32)
    value_grad = jnp.zeros(values.shape, F32)
    for head_index in range(queries.shape[1]):
        query_head = queries[:, head_index]
        grad_head = out_grad[:, head_index]
        scores = inner_cols(query_head, key_rows) * score_scale
        scores = jnp.where(allowed, scores, NEG)
        probs = jnp.exp(scores - logsums[:, head_index])
        value_grad = value_grad + inner_rows(probs.astype(BF), grad_head)
        prob_grad = inner_cols(grad_head, values)
        weighted = jnp.sum(probs * prob_grad, axis=-1, keepdims=True)
        score_grad = (probs * (prob_grad - weighted)).astype(BF)
        query_grads.append(matmul(score_grad, key_rows) * score_scale)
        key_grad = key_grad + inner_rows(score_grad, query_head) * score_scale
    return (jnp.stack(query_grads, axis=1), key_grad, value_grad)


def kernel_call(body, outs, args, flops, scratch=(), smem=()):
    nbytes = sum(a.size * a.dtype.itemsize for a in args)
    nbytes += sum(o.size * o.dtype.itemsize for o in outs)
    vmem = pl.BlockSpec(memory_space=pltpu.VMEM)
    return pl.pallas_call(
        body,
        out_shape=outs,
        in_specs=[
            pl.BlockSpec(memory_space=pltpu.SMEM) if i in smem else vmem for i in range(len(args))
        ],
        out_specs=[vmem] * len(outs),
        scratch_shapes=list(scratch),
        compiler_params=pltpu.CompilerParams(vmem_limit_bytes=48 * 1024 * 1024),
        cost_estimate=pl.CostEstimate(flops=flops, bytes_accessed=nbytes, transcendentals=0),
    )(*args)


def shape(dims, kind):
    return jax.ShapeDtypeStruct(dims, kind)


def rms_scale(value):
    return lax.rsqrt(jnp.mean(value * value, axis=-1, keepdims=True) + EPS)


def rms_back(value, inverse, gain, grad):
    scaled = value * inverse
    gain_grad = jnp.sum(grad * scaled, axis=0, keepdims=True)
    weighted = grad * gain
    mean = jnp.mean(weighted * scaled, axis=-1, keepdims=True)
    return inverse * (weighted - scaled * mean), gain_grad


def rows_at(start, size, step):
    return pl.ds(pl.multiple_of(start, step), size)


def key_value(inputs, blocks, norm_in, norm_key, cosine, sine, block_ids):
    rows, width = inputs.shape
    size = norm_key.shape[1]
    shard = width // 4

    def body(x, w0, w1, w2, w3, g_in, g_key, cos, sin, ids, hidden, key_pre, packed, full):
        place = lax.axis_index("fsdp")
        for flip, block in enumerate((w0, w1, w2, w3)):
            full[rows_at((place ^ flip) * shard, shard, 16), :] = block[:shard, :]
        value = x[...].astype(F32)
        hid = (value * rms_scale(value) * g_in[...]).astype(BF)
        hidden[...] = hid
        both = matmul(hid, full[...])
        key = both[:, :size]
        key_pre[...] = key
        turned = rotate(key * rms_scale(key) * g_key[...], cos[...], sin[...])
        packed[:rows, :size] = turned.astype(BF)
        packed[:rows, size:] = both[:, size:].astype(BF)
        row = lax.broadcasted_iota(jnp.int32, (16, 2 * size), 0)
        packed[rows:, :] = jnp.where(row == 0, ids[0, 0], ids[0, 1]).astype(F32).astype(BF)

    outs = [
        shape((rows, width), BF),
        shape((rows, size), F32),
        shape((rows + 16, 2 * size), BF),
        shape((width, 2 * size), BF),
    ]
    args = [inputs, *blocks, norm_in, norm_key, cosine, sine, block_ids]
    return kernel_call(body, outs, args, 4 * rows * width * size, smem=(9,))


def query(hidden, mine, other, norm_query, cosine, sine):
    rows, width = hidden.shape
    size = norm_query.shape[1]
    part, cols = mine[0].shape
    heads = cols // size

    def body(hid, *refs):
        blocks, (g_query, cos, sin, query_pre, queries, full) = refs[:8], refs[8:]
        place = lax.axis_index("fsdp")
        core = lax.axis_index("seq")
        for flip in range(4):
            start = (place ^ flip) * 2
            full[rows_at((start + core) * part, part, 16), :] = blocks[flip][...]
            full[rows_at((start + 1 - core) * part, part, 16), :] = blocks[4 + flip][...]
        for head in range(heads):
            at = slice(head * size, (head + 1) * size)
            value = matmul(hid[...], full[:, at])
            query_pre[:, at] = value
            turned = rotate(value * rms_scale(value) * g_query[...], cos[...], sin[...])
            queries[head] = turned.astype(BF)

    outs = [
        shape((rows, cols), F32),
        shape((heads, rows, size), BF),
        shape((width, cols), BF),
    ]
    args = [hidden, *mine, *other, norm_query, cosine, sine]
    return kernel_call(body, outs, args, 2 * rows * width * cols)


def tile_masks(blocks, rows):
    half = rows // 2
    lane = lax.broadcasted_iota(jnp.int32, (1, half), 1).astype(F32)
    row = lax.broadcasted_iota(jnp.int32, (rows, 1), 0)
    own = blocks[0][rows : rows + 16, :half].astype(F32)
    low, high = own[0:1, 0:1], own[1:2, 0:1]
    query_order = jnp.where(row < half, low, high) * half
    query_order = query_order + jnp.where(row < half, row, row - half).astype(F32)
    masks = []
    for block in blocks:
        ids = block[rows : rows + 16, :half].astype(F32)
        keys = jnp.concatenate([ids[0:1] * half + lane, ids[1:2] * half + lane], 1)
        masks.append(keys <= query_order)
    return masks


def attend_kernel(queries, kv_blocks, score_scale):
    heads, rows, size = queries.shape
    count = len(kv_blocks)

    def body(*refs):
        q, blocks, (context, logsum) = refs[0], refs[1 : 1 + count], refs[1 + count :]
        masks = tile_masks(blocks, rows)
        for head in range(heads):
            scores = [
                jnp.where(mask, inner_cols(q[head], block[:rows, :size]) * score_scale, NEG)
                for block, mask in zip(blocks, masks)
            ]
            highest = scores[0].max(-1, keepdims=True)
            for tile in scores[1:]:
                highest = jnp.maximum(highest, tile.max(-1, keepdims=True))
            weights = [jnp.exp(tile - highest) for tile in scores]
            summed = sum(tile.sum(-1, keepdims=True) for tile in weights)
            inverse = 1.0 / summed
            out = sum(
                matmul((tile * inverse).astype(BF), block[:rows, size:])
                for tile, block in zip(weights, blocks)
            )
            context[head] = out.astype(BF)
            logsum[head] = highest + jnp.log(summed)

    outs = [shape((heads, rows, size), BF), shape((heads, rows, 1), F32)]
    return kernel_call(body, outs, [queries, *kv_blocks], 4 * heads * rows * rows * count * size)


def attend_back_kernel(queries, kv_blocks, logsum, out_grad, score_scale):
    heads, rows, size = queries.shape
    count = len(kv_blocks)

    def body(*refs):
        q, blocks, refs = refs[0], refs[1 : 1 + count], refs[1 + count :]
        lse, grads, query_grad, kv_grads, kv_acc = refs[0], refs[1], refs[2], refs[3:-1], refs[-1]
        masks = tile_masks(blocks, rows)
        for head in range(heads):
            q_head, g_head = q[head], grads[head]
            low = lse[head]
            probs = [
                jnp.exp(
                    jnp.where(mask, inner_cols(q_head, block[:rows, :size]) * score_scale, NEG)
                    - low
                )
                for block, mask in zip(blocks, masks)
            ]
            prob_grads = [inner_cols(g_head, block[:rows, size:]) for block in blocks]
            weighted = sum(
                (a * b).sum(-1, keepdims=True) for a, b in zip(probs, prob_grads)
            )
            total = None
            for i, (prob, grad, block) in enumerate(zip(probs, prob_grads, blocks)):
                score_grad = (prob * (grad - weighted)).astype(BF)
                part = matmul(score_grad, block[:rows, :size])
                total = part if total is None else total + part
                key_part = inner_rows(score_grad, q_head) * score_scale
                value_part = inner_rows(prob.astype(BF), g_head)
                if head == 0:
                    kv_acc[i, :, :size] = key_part
                    kv_acc[i, :, size:] = value_part
                else:
                    kv_acc[i, :, :size] += key_part
                    kv_acc[i, :, size:] += value_part
            query_grad[head] = total * score_scale
        for i in range(count):
            kv_grads[i][...] = kv_acc[i].astype(BF)

    outs = [shape((heads, rows, size), F32)] + [shape((rows, 2 * size), BF)] * count
    return kernel_call(
        body,
        outs,
        [queries, *kv_blocks, logsum, out_grad],
        10 * heads * rows * rows * count * size,
        scratch=[pltpu.VMEM((count, rows, 2 * size), F32)],
    )


def gelu_parts(value):
    scale = (2.0 / jnp.pi) ** 0.5
    square = value * value
    tanh = jnp.tanh(scale * (value + 0.044715 * square * value))
    half = 0.5 * (1.0 + tanh)
    slope = half + 0.5 * value * (1.0 - tanh * tanh) * scale * (1.0 + 3 * 0.044715 * square)
    return value * half, slope


def feed_forward(
    inputs, cotangent, context, out_mine, out_other, gate_up, down, norm_attn, norm_pre, norm_post
):
    heads, rows, size = context.shape
    width = inputs.shape[1]
    unit = down[0].shape[0]
    half = size // 2
    count = len(down)
    hidden = unit * count // 2
    offs = [0, width, 2 * width, 3 * width]
    offs += [offs[3] + hidden, offs[3] + 2 * hidden, offs[3] + 3 * hidden]
    total_cols = offs[6] + heads * half

    def body(x, cot, ctx, *refs):
        om, oo, gu, dn = refs[:4], refs[4:8], refs[8 : 8 + count], refs[8 + count : 8 + 2 * count]
        refs = refs[8 + 2 * count :]
        g_attn, g_pre, g_post = refs[0][...], refs[1][...], refs[2][...]
        result, middle_grad, own, send, ctx_grad, gain_grads = refs[3:9]
        w_out, gate, up = refs[9:]
        place = lax.axis_index("fsdp")
        core = lax.axis_index("seq")
        attn_out = None
        for flip in range(4):
            w_out[flip, rows_at(core * half, half, 16), :] = om[flip][...]
            w_out[flip, rows_at((1 - core) * half, half, 16), :] = oo[flip][...]
            value = ctx[place ^ flip]
            low, high = value[:, :half], value[:, half:]
            at = slice(offs[6] + flip * half, offs[6] + (flip + 1) * half)
            own[:, at] = jnp.where(core == 0, low, high)
            send[:, at] = jnp.where(core == 0, high, low)
            part = matmul(value, w_out[flip])
            attn_out = part if attn_out is None else attn_out + part
        inv_attn = rms_scale(attn_out)
        middle = x[...].astype(F32) + attn_out * inv_attn * g_attn
        inv_pre = rms_scale(middle)
        ffn_in = (middle * inv_pre * g_pre).astype(BF)
        own[:, : offs[1]] = ffn_in
        send[:, : offs[1]] = ffn_in
        ffn_out = None
        for i in range(count):
            pre = matmul(ffn_in, gu[i][...])
            gate_pre, up_pre = pre[:, :unit], pre[:, unit:]
            gate[i] = gate_pre
            up[i] = up_pre
            mixed = (gelu_parts(gate_pre)[0] * up_pre).astype(BF)
            j = i % (count // 2)
            dest = own if i < count // 2 else send
            dest[:, offs[3] + j * unit : offs[3] + (j + 1) * unit] = mixed
            part = matmul(mixed, dn[i][...])
            ffn_out = part if ffn_out is None else ffn_out + part
        inv_post = rms_scale(ffn_out)
        result[...] = middle + ffn_out * inv_post * g_post
        grad = cot[...].astype(F32)
        ffn_grad, post_grad = rms_back(ffn_out, inv_post, g_post, grad)
        ffn_grad = ffn_grad.astype(BF)
        own[:, offs[1] : offs[2]] = ffn_grad
        send[:, offs[1] : offs[2]] = ffn_grad
        pre_total = None
        for i in range(count):
            mixed_grad = inner_cols(ffn_grad, dn[i][...])
            activated, slope = gelu_parts(gate[i])
            gate_grad = (mixed_grad * up[i] * slope).astype(BF)
            up_grad = (mixed_grad * activated).astype(BF)
            j = i % (count // 2)
            dest = own if i < count // 2 else send
            dest[:, offs[4] + j * unit : offs[4] + (j + 1) * unit] = gate_grad
            dest[:, offs[5] + j * unit : offs[5] + (j + 1) * unit] = up_grad
            part = inner_cols(gate_grad, gu[i][:, :unit]) + inner_cols(up_grad, gu[i][:, unit:])
            pre_total = part if pre_total is None else pre_total + part
        part, pre_grad = rms_back(middle, inv_pre, g_pre, pre_total)
        mid_grad = grad + part
        middle_grad[...] = mid_grad
        attn_grad, attn_gain = rms_back(attn_out, inv_attn, g_attn, mid_grad)
        attn_grad = attn_grad.astype(BF)
        own[:, offs[2] : offs[3]] = attn_grad
        send[:, offs[2] : offs[3]] = attn_grad
        for flip in range(4):
            ctx_grad[place ^ flip] = inner_cols(attn_grad, w_out[flip]).astype(BF)
        gain_grads[...] = jnp.concatenate(
            [attn_gain, pre_grad, post_grad, jnp.zeros((5, width), F32)], 0
        )

    outs = [
        shape((rows, width), F32),
        shape((rows, width), F32),
        shape((rows, total_cols), BF),
        shape((rows, total_cols), BF),
        shape((heads, rows, size), BF),
        shape((8, width), F32),
    ]
    args = [inputs, cotangent, context, *out_mine, *out_other, *gate_up, *down]
    args += [norm_attn, norm_pre, norm_post]
    scratch = [
        pltpu.VMEM((4, size, width), BF),
        pltpu.VMEM((count, rows, unit), F32),
        pltpu.VMEM((count, rows, unit), F32),
    ]
    flops = 2 * rows * width * (6 * unit * count + 2 * heads * size)
    return kernel_call(body, outs, args, flops, scratch), offs


def ffn_weight_grads(own, got, offs, unit, half):
    rows = own.shape[0]
    width = offs[1]

    def body(a, b, *outs):
        def product(left, right):
            return (
                inner_rows(a[:, left], a[:, right]) + inner_rows(b[:, left], b[:, right])
            ).astype(BF)

        at = lambda k, j, size: slice(offs[k] + j * size, offs[k] + (j + 1) * size)
        whole = lambda k: slice(offs[k], offs[k] + width)
        for j in range(4):
            rest, gate_up = outs[j], outs[4 + j]
            rest[:unit, :] = product(at(3, j, unit), whole(1))
            rest[unit:, :] = product(at(6, j, half), whole(2))
            gate_up[:, :unit] = product(whole(0), at(4, j, unit))
            gate_up[:, unit:] = product(whole(0), at(5, j, unit))

    outs = [shape((unit + half, width), BF)] * 4 + [shape((width, 2 * unit), BF)] * 4
    flops = 4 * rows * width * 4 * (3 * unit + half)
    return kernel_call(body, outs, [own, got], flops)


def query_back(query_grad, query_pre, norm_query, cosine, sine, query_full):
    heads, rows, size = query_grad.shape
    width = query_full.shape[0]
    per = heads // 2

    def body(grad, pre, g_query, cos, sin, full, hidden_part, mine, other, gain_grad):
        core = lax.axis_index("seq")
        gains = None
        outs = []
        total = None
        for head in range(heads):
            at = slice(head * size, (head + 1) * size)
            value = pre[:, at]
            turned = rotate(grad[head], cos[...], -sin[...])
            back, gain = rms_back(value, rms_scale(value), g_query[...], turned)
            gains = gain if gains is None else gains + gain
            outs.append(back.astype(BF))
            part = inner_cols(outs[-1], full[:, at])
            total = part if total is None else total + part
        hidden_part[...] = total
        for head in range(per):
            at = slice(head * size, (head + 1) * size)
            mine[:, at] = jnp.where(core == 0, outs[head], outs[per + head])
            other[:, at] = jnp.where(core == 0, outs[per + head], outs[head])
        gain_grad[...] = gains

    outs = [
        shape((rows, width), F32),
        shape((rows, per * size), BF),
        shape((rows, per * size), BF),
        shape((1, size), F32),
    ]
    args = [query_grad, query_pre, norm_query, cosine, sine, query_full]
    return kernel_call(body, outs, args, 2 * rows * width * heads * size)


def input_back(
    kv_back, key_pre, norm_key, cosine, sine, kv_full, hidden_part, inputs, norm_in, middle_grad,
    hidden, query_mine, query_other,
):
    rows, width = inputs.shape
    size = norm_key.shape[1]
    per = query_mine.shape[1]
    cols = width + per + size

    def body(
        back, k_pre, g_key, cos, sin, full, part, x, g_in, mid, hid, q_mine, q_other,
        input_grad, own, send, in_gain, key_gain,
    ):
        core = lax.axis_index("seq")
        value = k_pre[...]
        turned = rotate(back[:, :size], cos[...], -sin[...])
        key_grad, gain = rms_back(value, rms_scale(value), g_key[...], turned)
        key_gain[...] = gain
        key_grad = key_grad.astype(BF)
        value_grad = back[:, size:].astype(BF)
        total = part[...] + inner_cols(key_grad, full[:, :size])
        total = total + inner_cols(value_grad, full[:, size:])
        value = x[...].astype(F32)
        grad, gain = rms_back(value, rms_scale(value), g_in[...], total)
        input_grad[...] = mid[...] + grad
        in_gain[...] = gain
        own[:, :width] = hid[...]
        send[:, :width] = hid[...]
        own[:, width : width + per] = q_mine[...]
        send[:, width : width + per] = q_other[...]
        own[:, width + per :] = jnp.where(core == 0, key_grad, value_grad)
        send[:, width + per :] = jnp.where(core == 0, value_grad, key_grad)

    outs = [
        shape((rows, width), F32),
        shape((rows, cols), BF),
        shape((rows, cols), BF),
        shape((1, width), F32),
        shape((1, size), F32),
    ]
    args = [kv_back, key_pre, norm_key, cosine, sine, kv_full, hidden_part, inputs, norm_in]
    args += [middle_grad, hidden, query_mine, query_other]
    return kernel_call(body, outs, args, 4 * rows * width * size)


def late_grads(own, got, gains, width):
    rows, cols = own.shape
    out_cols = cols - width
    shard = width // 4

    def body(a, b, extra, *refs):
        outs, total = refs[:4], refs[4]
        place = lax.axis_index("fsdp")
        total[...] = inner_rows(a[:, :width], a[:, width:]) + inner_rows(b[:, :width], b[:, width:])
        for flip, out in enumerate(outs):
            out[:shard, :] = total[rows_at((place ^ flip) * shard, shard, 16), :].astype(BF)
            out[shard:, :] = extra[place ^ flip]

    outs = [shape((shard + gains.shape[1], out_cols), BF)] * 4
    flops = 4 * rows * width * out_cols
    scratch = [pltpu.VMEM((width, out_cols), F32)]
    return kernel_call(body, outs, [own, got, gains], flops, scratch)


def pick_half(value, which, axis):
    size = value.shape[axis] // 2
    return lax.dynamic_slice_in_dim(value, which * size, size, axis)


def join_cols(mine, other, core):
    return jnp.where(
        core == 0, jnp.concatenate([mine, other], 1), jnp.concatenate([other, mine], 1)
    ).astype(F32)


def after(value, *others):
    return lax.optimization_barrier((value,) + others)[0]


def on_device(ctx_size):
    def run(
        inputs,
        positions,
        block_ids,
        w_query,
        w_key,
        w_value,
        w_out,
        w_gate,
        w_up,
        w_down,
        gain_in,
        gain_query,
        gain_key,
        gain_attn,
        gain_pre,
        gain_post,
        cotangent,
    ):
        core = lax.axis_index("seq")
        fsdp = lax.axis_index("fsdp")
        seq_rows, model_width = inputs.shape[1:]
        head_size = gain_query.shape[0] * 4
        half_rows = seq_rows // 2
        score_scale = head_size ** (-0.5)
        inputs, cotangent = inputs[0], cotangent[0]

        gains = [gain_in, gain_attn, gain_pre, gain_post, gain_query, gain_key]
        gain_sizes = [member.shape[0] for member in gains]
        kv_width = 2 * head_size
        shard_rows = w_key.shape[0]
        gain_row = jnp.concatenate(gains)
        gain_row = jnp.pad(gain_row, (0, 16 * kv_width - gain_row.shape[0]))
        packed = jnp.concatenate(
            [jnp.concatenate([w_key, w_value], 1), gain_row.reshape(16, kv_width)], 0
        )
        first = [packed] + [swap(packed, "fsdp", flip, 4) for flip in (1, 2, 3)]
        used = -(-sum(gain_sizes) // kv_width)
        rows = [block[shard_rows : shard_rows + used].astype(F32) for block in first]
        placed = []
        for index in range(4):
            row = rows[0]
            for flip in range(1, 4):
                row = jnp.where((fsdp ^ flip) == index, rows[flip], row)
            placed.append(row.reshape(-1))
        placed = jnp.stack(placed, 0)
        norms = []
        start = 0
        for size in gain_sizes:
            norms.append(placed[:, start : start + size].reshape(1, -1))
            start += size
        norm_in, norm_attn, norm_pre, norm_post, norm_query, norm_key = norms

        def fetch(mine, other):
            mine = gather4(mine, core, "fsdp", 4, 1, 2)
            return mine, [other] + [swap_pair(block) for block in mine[1:]]

        def fetch_half(shard, *order):
            mine, other = pick_half(shard, core, 0), pick_half(shard, 1 - core, 0)
            return fetch(after(mine, *order), other)

        query_mine, query_other = fetch_half(w_query, first[3])
        out_mine, out_other = fetch_half(w_out, query_mine[1], query_mine[2])
        gate_up = jnp.concatenate([pick_half(w_gate, core, 1), pick_half(w_up, core, 1)], 1)
        gate_up_other = jnp.concatenate(
            [pick_half(w_gate, 1 - core, 1), pick_half(w_up, 1 - core, 1)], 1
        )
        gu_mine, gu_other = fetch(after(gate_up, out_mine[1], out_mine[2]), gate_up_other)
        down_mine, down_other = fetch_half(w_down, gu_mine[1], gu_mine[2])
        unit = gate_up.shape[1] // 2

        cosine, sine = tables(positions[0], head_size)
        hidden, key_pre, packed_kv, kv_full = key_value(
            inputs, first, norm_in, norm_key, cosine, sine, block_ids
        )
        if ctx_size == 4:
            kv_blocks = gather4(packed_kv, core, "ctx", 4, 1, 3)
        else:
            kv_all = lax.all_gather(packed_kv, "ctx", axis=0)
        query_pre, queries, query_full = query(
            hidden, query_mine, query_other, norm_query, cosine, sine
        )
        if ctx_size == 4:
            context, logsum = attend_kernel(queries, kv_blocks, score_scale)
        else:
            offsets = jnp.arange(half_rows, dtype=jnp.int32)
            block_all = kv_all[:, seq_rows : seq_rows + 2, 0].astype(jnp.int32)
            key_order = (block_all[:, :, None] * half_rows + offsets).reshape(-1)
            query_order = (block_ids[0][:, None] * half_rows + offsets).reshape(-1)
            key_all = kv_all[:, :seq_rows, :head_size].reshape(-1, head_size)
            value_all = kv_all[:, :seq_rows, head_size:].reshape(-1, head_size)
            by_row = queries.transpose(1, 0, 2)
            seq_out, logsum = attend_forward(
                by_row, key_all, value_all, query_order, key_order, score_scale
            )
            context = seq_out.astype(BF).transpose(1, 0, 2)

        (result, middle_grad, own, send, context_grad, gain_grads), offs = feed_forward(
            inputs,
            cotangent,
            context,
            out_mine,
            out_other,
            gu_mine + gu_other,
            down_mine + down_other,
            norm_attn,
            norm_pre,
            norm_post,
        )

        parts = ffn_weight_grads(own, swap_pair(send), offs, unit, head_size // 2)
        rest_sum = ctx_sum(scatter4(parts[:4], core, "fsdp", 4, 1, 2), ctx_size, 1)
        gu_sum = ctx_sum(scatter4(parts[4:], core, "fsdp", 4, 1, 2), ctx_size, 0)
        rest_other = swap_pair(rest_sum)
        gu_other = swap_pair(gu_sum)
        total_down = join(rest_sum[:unit], rest_other[:unit], core).astype(F32)
        total_out = join(rest_sum[unit:], rest_other[unit:], core).astype(F32)
        total_gate = join_cols(gu_sum[:, :unit], gu_other[:, :unit], core)
        total_up = join_cols(gu_sum[:, unit:], gu_other[:, unit:], core)

        context_grad = after(context_grad, *parts)
        if ctx_size == 4:
            query_grad, *kv_parts = attend_back_kernel(
                queries, kv_blocks, logsum, context_grad, score_scale
            )
            kv_back = scatter4(kv_parts, core, "ctx", 4, 1, 3)
        else:
            query_grad, key_grad, value_grad = attend_backward(
                by_row,
                key_all,
                value_all,
                query_order,
                key_order,
                score_scale,
                logsum,
                context_grad.transpose(1, 0, 2),
            )
            query_grad = query_grad.transpose(1, 0, 2)
            kv_grad = jnp.concatenate([key_grad, value_grad], 1).astype(BF)
            kv_back = lax.psum_scatter(kv_grad, "ctx", scatter_dimension=0, tiled=True).astype(F32)
        hidden_part, back_mine, back_other, grad_query = query_back(
            query_grad, query_pre, norm_query, cosine, sine, query_full
        )
        input_grad, own, send, grad_in, grad_key = input_back(
            kv_back,
            key_pre,
            norm_key,
            cosine,
            sine,
            kv_full,
            hidden_part,
            inputs,
            norm_in,
            middle_grad,
            hidden,
            back_mine,
            back_other,
        )
        gain_list = (grad_in, gain_grads[0], gain_grads[1], gain_grads[2], grad_query, grad_key)
        gain_rows = jnp.concatenate([member.reshape(4, 1, -1) for member in gain_list], 2)
        width = own.shape[1] - model_width
        gain_count = -(-gain_rows.shape[2] // width)
        gain_rows = jnp.pad(gain_rows, ((0, 0), (0, 0), (0, gain_count * width - gain_rows.shape[2])))
        gain_rows = gain_rows.reshape(4, gain_count, width).astype(BF)
        gain_rows = jnp.pad(gain_rows, ((0, 0), (0, 32 - gain_count), (0, 0)))
        late_parts = late_grads(own, swap_pair(send), gain_rows, model_width)
        late_sum = ctx_sum(scatter4(late_parts, core, "fsdp", 4, 1, 2), ctx_size, 0)
        late_other = swap_pair(late_sum)
        query_cols = width - head_size
        total_query = join_cols(
            late_sum[:shard_rows, :query_cols], late_other[:shard_rows, :query_cols], core
        )
        total_key = jnp.where(core == 0, late_sum, late_other)[:shard_rows, query_cols:].astype(F32)
        total_value = jnp.where(core == 0, late_other, late_sum)[:shard_rows, query_cols:].astype(F32)
        gain_at = slice(shard_rows, shard_rows + gain_count)
        gain_total = (late_sum[gain_at].astype(F32) + late_other[gain_at].astype(F32)).reshape(-1)
        outs = []
        start = 0
        for size in gain_sizes:
            outs.append(gain_total[start : start + size])
            start += size
        g_in, g_attn, g_pre, g_post, g_query, g_key = outs
        return (
            result[None],
            input_grad[None],
            total_query,
            total_key,
            total_value,
            total_out,
            total_gate,
            total_up,
            total_down,
            g_in,
            g_query,
            g_key,
            g_attn,
            g_pre,
            g_post,
        )

    return run


def solution(mesh):
    rows = P(("seq", "fsdp"), "ctx")
    wide = P(("seq", "fsdp"), "ctx", None)
    first = P("fsdp", None)
    second = P(None, "fsdp")
    flat = P("fsdp")
    in_specs = (wide, rows, rows, first, first, first, first, second, second, first)
    in_specs += (flat,) * 6 + (wide,)
    out_specs = (wide, wide, first, first, first, first, second, second, first) + (flat,) * 6
    return jax.shard_map(
        on_device(mesh.shape["ctx"]),
        mesh=mesh,
        in_specs=in_specs,
        out_specs=out_specs,
        check_vma=False,
    )
```

```python
import jax
import jax.numpy as jnp
from jax import lax
from jax.experimental import pallas as pl
from jax.experimental.pallas import tpu as pltpu
from jax.sharding import PartitionSpec as P

EPS = 1e-06
THETA = 1000000.0
NEG = -1e30
BF = jnp.bfloat16
F32 = jnp.float32


def matmul(left, right):
    return jnp.dot(left, right, preferred_element_type=F32)


def inner_cols(left, right):
    return lax.dot_general(left, right, (((1,), (1,)), ((), ())), preferred_element_type=F32)


def inner_rows(left, right):
    return lax.dot_general(left, right, (((0,), (0,)), ((), ())), preferred_element_type=F32)


def rotate(value, cosine, sine_table):
    half = value.shape[-1] // 2
    first = value[..., :half]
    second = value[..., half:]
    return jnp.concatenate(
        [first * cosine - second * sine_table, second * cosine + first * sine_table], axis=-1
    )


def tables(positions, head_size):
    half = head_size // 2
    freq = 1.0 / THETA ** (jnp.arange(half, dtype=F32) * 2.0 / head_size)
    angle = positions.astype(F32)[:, None] * freq[None, :]
    return (jnp.cos(angle), jnp.sin(angle))


def swap(value, axis, flip, size):
    return lax.ppermute(value, axis, [(i, i ^ flip) for i in range(size)])


def swap_pair(value):
    return swap(value, "seq", 1, 2)


def swap_split(value, axis, size, flip0, flip1):
    perm = [(i, i ^ flip0) for i in range(size)]
    perm += [(size + i, size + (i ^ flip1)) for i in range(size)]
    return lax.ppermute(value, ("seq", axis), perm)


def scatter4(blocks, via, core, axis, size, first, second, order):
    via = via.astype(F32)
    none = jnp.zeros_like(via)
    one = (blocks[1].astype(F32) + jnp.where(core == 0, via, none)).astype(BF)
    two = (blocks[2].astype(F32) + jnp.where(core == 0, none, via)).astype(BF)
    one = swap(order(one), axis, first, size).astype(F32)
    two = swap(order(two), axis, second, size).astype(F32)
    return blocks[0].astype(F32) + one + two


def halves(value, pick):
    axis = value.ndim - 2
    rows = value.shape[axis] // 2
    keep = lax.dynamic_slice_in_dim(value, pick * rows, rows, axis)
    send = lax.dynamic_slice_in_dim(value, (1 - pick) * rows, rows, axis)
    return keep, send


def join(mine, other, pick):
    return jnp.where(
        pick == 0, jnp.concatenate([mine, other], 0), jnp.concatenate([other, mine], 0)
    )


class Order:
    def __init__(self):
        self.last = None

    def __call__(self, value):
        if self.last is not None:
            value = lax.optimization_barrier((value, self.last))[0]
        self.last = value
        return value

    def wait(self, value):
        return lax.optimization_barrier((value, self.last))[0]


def reduce_steps(blocks, core, ctx_size, cuts, order):
    place = lax.axis_index("ctx")
    high = place // 2
    odd = lax.rem(place, 2)
    mixed = lax.rem(high + odd, 2)
    steps = [(1, mixed), (3, high)]
    via = swap_split(order(blocks[3]), "fsdp", 4, 2, 1)
    yield
    via = order.wait(via).astype(F32)
    none = jnp.zeros_like(via)
    one = (blocks[1].astype(F32) + jnp.where(core == 0, via, none)).astype(BF)
    two = (blocks[2].astype(F32) + jnp.where(core == 0, none, via)).astype(BF)
    one = swap(order(one), "fsdp", 1, 4)
    two = swap(order(two), "fsdp", 2, 4)
    yield
    one, two = order.wait(one), order.wait(two)
    value = blocks[0].astype(F32) + one.astype(F32) + two.astype(F32)
    if ctx_size != 4:
        value = lax.psum(value.astype(BF), "ctx")
    elif not cuts:
        for flip in (1, 3):
            value = value.astype(BF)
            got = swap(order(value), "ctx", flip, 4)
            yield
            value = value.astype(F32) + order.wait(got).astype(F32)
        value = value.astype(BF)
    pieces = [value]
    if cuts:
        edges = [0, *cuts, value.shape[1]]
        pieces = [value[:, a:b] for a, b in zip(edges, edges[1:])]
    if cuts and ctx_size == 4:
        turns = [steps, steps[::-1]]
        for k in range(2):
            got, keep = [], []
            for piece, turn in zip(pieces, turns):
                flip, pick = turn[k]
                kept, send = halves(piece, pick)
                keep.append(kept)
                got.append(swap(order(send.astype(BF)), "ctx", flip, 4))
            yield
            pieces = [a.astype(F32) + order.wait(b).astype(F32) for a, b in zip(keep, got)]
        pieces = [piece.astype(BF) for piece in pieces]
        for k in (1, 0):
            got = [swap(order(p), "ctx", turn[k][0], 4) for p, turn in zip(pieces, turns)]
            yield
            pieces = [
                join(p, order.wait(b), turn[k][1]) for p, b, turn in zip(pieces, got, turns)
            ]
    others = [swap_pair(order(piece)) for piece in pieces]
    yield
    yield pieces, others


def attend_forward(queries, key_rows, values, query_order, key_order, score_scale):
    allowed = key_order[None, :] <= query_order[:, None]
    outputs = []
    logsums = []
    for head_index in range(queries.shape[1]):
        scores = inner_cols(queries[:, head_index], key_rows) * score_scale
        scores = jnp.where(allowed, scores, NEG)
        highest = jnp.max(scores, axis=-1, keepdims=True)
        weights = jnp.exp(scores - highest)
        summed = jnp.sum(weights, axis=-1, keepdims=True)
        probs = (weights / summed).astype(BF)
        outputs.append(matmul(probs, values))
        logsums.append(highest + jnp.log(summed))
    return (jnp.stack(outputs, axis=1), jnp.stack(logsums, axis=1))


def attend_backward(
    queries, key_rows, values, query_order, key_order, score_scale, logsums, out_grad
):
    allowed = key_order[None, :] <= query_order[:, None]
    query_grads = []
    key_grad = jnp.zeros(key_rows.shape, F32)
    value_grad = jnp.zeros(values.shape, F32)
    for head_index in range(queries.shape[1]):
        query_head = queries[:, head_index]
        grad_head = out_grad[:, head_index]
        scores = inner_cols(query_head, key_rows) * score_scale
        scores = jnp.where(allowed, scores, NEG)
        probs = jnp.exp(scores - logsums[:, head_index])
        value_grad = value_grad + inner_rows(probs.astype(BF), grad_head)
        prob_grad = inner_cols(grad_head, values)
        weighted = jnp.sum(probs * prob_grad, axis=-1, keepdims=True)
        score_grad = (probs * (prob_grad - weighted)).astype(BF)
        query_grads.append(matmul(score_grad, key_rows) * score_scale)
        key_grad = key_grad + inner_rows(score_grad, query_head) * score_scale
    return (jnp.stack(query_grads, axis=1), key_grad, value_grad)


class Waiting:
    def __init__(self, ref, copy):
        self.ref, self.copy = ref, copy

    def wait(self):
        if self.copy is not None:
            self.copy.wait()
            self.copy = None

    def __getitem__(self, index):
        self.wait()
        return self.ref[index]


def kernel_call(body, outs, args, flops, scratch=(), smem=(), far=(), back=(), room=16, flushes=0):
    nbytes = sum(a.size * a.dtype.itemsize for a in args)
    nbytes += sum(o.size * o.dtype.itemsize for o in outs)
    hbm = pl.BlockSpec(memory_space=pltpu.HBM)
    specs = {i: hbm for i in far}
    specs.update({i: pl.BlockSpec(memory_space=pltpu.SMEM) for i in smem})
    n_in, n_out, n_own = len(args), len(outs), len(scratch)

    def wrapped(*refs):
        ins, dests = list(refs[:n_in]), list(refs[n_in : n_in + n_out])
        rest = refs[n_in + n_out :]
        own, rest = rest[:n_own], rest[n_own:]
        sems = rest[-1]
        for k, i in enumerate(far):
            copy = pltpu.make_async_copy(ins[i], rest[k], sems.at[k])
            copy.start()
            ins[i] = Waiting(rest[k], copy)
        kept = list(dests)
        for k, i in enumerate(back):
            kept[i] = rest[len(far) + k]
        copies = []
        flushed = set()

        def flush(which, cols):
            at = (slice(None), cols)
            sem = sems.at[len(far) + len(back) + len(copies)]
            copies.append(pltpu.make_async_copy(kept[which].at[at], dests[which].at[at], sem))
            copies[-1].start()
            flushed.add(which)

        body(*ins, *kept, *own, *([flush] if flushes else []))
        for k, i in enumerate(back):
            if i in flushed:
                continue
            copies.append(pltpu.make_async_copy(kept[i], dests[i], sems.at[len(far) + k]))
            copies[-1].start()
        for i in far:
            ins[i].wait()
        for copy in copies:
            copy.wait()

    buffers = [pltpu.VMEM(args[i].shape, args[i].dtype) for i in far]
    buffers += [pltpu.VMEM(outs[i].shape, outs[i].dtype) for i in back]
    return pl.pallas_call(
        wrapped,
        out_shape=outs,
        in_specs=[specs.get(i, pl.BlockSpec()) for i in range(n_in)],
        out_specs=[hbm if i in back else pl.BlockSpec() for i in range(n_out)],
        scratch_shapes=list(scratch)
        + buffers
        + [pltpu.SemaphoreType.DMA((max(1, len(far) + len(back) + flushes),))],
        compiler_params=pltpu.CompilerParams(vmem_limit_bytes=room * 1024 * 1024),
        cost_estimate=pl.CostEstimate(flops=flops, bytes_accessed=nbytes, transcendentals=0),
    )(*args)


def shape(dims, kind):
    return jax.ShapeDtypeStruct(dims, kind)


def rms_scale(value):
    return lax.rsqrt(jnp.mean(value * value, axis=-1, keepdims=True) + EPS)


def rms_back(value, inverse, gain, grad):
    scaled = value * inverse
    gain_grad = jnp.sum(grad * scaled, axis=0, keepdims=True)
    weighted = grad * gain
    mean = jnp.mean(weighted * scaled, axis=-1, keepdims=True)
    return inverse * (weighted - scaled * mean), gain_grad


def rows_at(start, size, step):
    return pl.ds(pl.multiple_of(start, step), size)


def pack(w_query, w_key, w_value, gains):
    rows = w_query.shape[0] // 2
    widths = [w.shape[1] for w in (w_query, w_key, w_value)]
    total = sum(widths)

    def body(*refs):
        weights, (mine, other) = refs[:3], refs[-2:]
        core = lax.axis_index("seq")
        start = 0
        for ref, width in zip(weights, widths):
            at = slice(start, start + width)
            low, high = ref[:rows, :], ref[rows:, :]
            mine[:rows, at] = jnp.where(core == 0, low, high)
            other[:, at] = jnp.where(core == 0, high, low)
            start += width
        mine[rows:, :] = jnp.zeros((16, total), BF)
        for number, (ref, gain) in enumerate(zip(refs[3:-2], gains)):
            row = ref[...].astype(F32).reshape(1, gain.shape[0])
            mine[rows + number : rows + number + 1, : gain.shape[0]] = row.astype(BF)

    outs = [shape((rows + 16, total), BF), shape((rows, total), BF)]
    args = [w_query, w_key, w_value, *gains]
    return kernel_call(body, outs, args, 0, room=62)


def pack_ffn(w_gate, w_up, w_down, w_out):
    width = w_gate.shape[0]
    sizes = [w_gate.shape[1] // 2, w_up.shape[1] // 2, w_down.shape[0] // 2, w_out.shape[0] // 2]
    total = sum(sizes)

    def body(gate, up, down, out, mine, other):
        core = lax.axis_index("seq")
        start = 0
        for ref, size, turn in zip((gate, up, down, out), sizes, (False, False, True, True)):
            at = slice(start, start + size)
            low = ref[:size, :].T if turn else ref[:, :size]
            high = ref[size:, :].T if turn else ref[:, size:]
            mine[:, at] = jnp.where(core == 0, low, high)
            other[:, at] = jnp.where(core == 0, high, low)
            start += size

    outs = [shape((width, total), BF)] * 2
    args = [w_gate, w_up, w_down, w_out]
    return kernel_call(body, outs, args, 0, room=62), sizes[0]


def project(inputs, mine, other, size, cosine, sine, block_ids):
    rows, width = inputs.shape
    part, total = other[0].shape
    cols = total - 2 * size
    heads = cols // size

    def body(x, *refs):
        blocks, refs = refs[:8], refs[8:]
        cos, sin, ids = refs[:3]
        hidden, key_pre, packed, query_pre, queries, full, wide, narrow = refs[3:]
        place = lax.axis_index("fsdp")
        core = lax.axis_index("seq")
        for flip in range(4):
            start = (place ^ flip) * 2
            full[rows_at((start + core) * part, part, 16), :] = blocks[flip][:part, :]
            full[rows_at((start + 1 - core) * part, part, 16), :] = blocks[4 + flip][:part, :]
        rows_of = [blocks[flip][part:, : width // 4].astype(F32) for flip in range(4)]
        for index in range(4):
            piece = rows_of[0]
            for flip in range(1, 4):
                piece = jnp.where((place ^ flip) == index, rows_of[flip], piece)
            wide[:, index * (width // 4) : (index + 1) * (width // 4)] = piece
            narrow[:, index * (size // 4) : (index + 1) * (size // 4)] = piece[:, : size // 4]
        g_in, g_query, g_key = wide[0:1, :], narrow[4:5, :], narrow[5:6, :]
        value = x[...].astype(F32)
        hid = (value * rms_scale(value) * g_in).astype(BF)
        hidden[...] = hid
        both = matmul(hid, full[:, cols:])
        key = both[:, :size]
        key_pre[...] = key
        turned = rotate(key * rms_scale(key) * g_key, cos[...], sin[...])
        packed[:rows, :size] = turned.astype(BF)
        packed[:rows, size:] = both[:, size:].astype(BF)
        row = lax.broadcasted_iota(jnp.int32, (16, 2 * size), 0)
        packed[rows:, :] = jnp.where(row == 0, ids[0, 0], ids[0, 1]).astype(F32).astype(BF)
        for head in range(heads):
            at = slice(head * size, (head + 1) * size)
            value = matmul(hid, full[:, at])
            query_pre[:, at] = value
            turned = rotate(value * rms_scale(value) * g_query, cos[...], sin[...])
            queries[head] = turned.astype(BF)

    outs = [
        shape((rows, width), BF),
        shape((rows, size), F32),
        shape((rows + 16, 2 * size), BF),
        shape((rows, cols), F32),
        shape((heads, rows, size), BF),
        shape((width, total), BF),
        shape((16, width), F32),
        shape((16, size), F32),
    ]
    args = [inputs, *mine, *other, cosine, sine, block_ids]
    flops = 2 * rows * width * total
    far = (0, 9, 10)
    return kernel_call(body, outs, args, flops, smem=(11,), far=far, back=(0, 1, 3, 5), room=62)


def tile_masks(blocks, rows):
    half = rows // 2
    lane = lax.broadcasted_iota(jnp.int32, (1, half), 1).astype(F32)
    row = lax.broadcasted_iota(jnp.int32, (rows, 1), 0)
    own = blocks[0][rows : rows + 16, :half].astype(F32)
    low, high = own[0:1, 0:1], own[1:2, 0:1]
    query_order = jnp.where(row < half, low, high) * half
    query_order = query_order + jnp.where(row < half, row, row - half).astype(F32)
    masks = []
    for block in blocks:
        ids = block[rows : rows + 16, :half].astype(F32)
        keys = jnp.concatenate([ids[0:1] * half + lane, ids[1:2] * half + lane], 1)
        masks.append(keys <= query_order)
    return masks


def attend_kernel(queries, kv_blocks, score_scale):
    heads, rows, size = queries.shape
    count = len(kv_blocks)

    def body(*refs):
        q, blocks, (context, logsum) = refs[0], refs[1 : 1 + count], refs[1 + count :]
        masks = tile_masks(blocks, rows)
        for head in range(heads):
            scores = [
                jnp.where(mask, inner_cols(q[head], block[:rows, :size]) * score_scale, NEG)
                for block, mask in zip(blocks, masks)
            ]
            highest = scores[0].max(-1, keepdims=True)
            for tile in scores[1:]:
                highest = jnp.maximum(highest, tile.max(-1, keepdims=True))
            weights = [jnp.exp(tile - highest) for tile in scores]
            summed = sum(tile.sum(-1, keepdims=True) for tile in weights)
            inverse = 1.0 / summed
            out = sum(
                matmul((tile * inverse).astype(BF), block[:rows, size:])
                for tile, block in zip(weights, blocks)
            )
            context[head] = out.astype(BF)
            logsum[head] = highest + jnp.log(summed)

    outs = [shape((heads, rows, size), BF), shape((heads, rows, 1), F32)]
    flops = 4 * heads * rows * rows * count * size
    far = tuple(range(1, 1 + count))
    return kernel_call(body, outs, [queries, *kv_blocks], flops, far=far, room=24)


def query_head_back(grad, value, gain, cosine, sine):
    turned = rotate(grad, cosine, -sine)
    back, gain_grad = rms_back(value, rms_scale(value), gain, turned)
    return back.astype(BF), gain_grad


def split_heads(parts, core, mine, other, size):
    per = len(parts) // 2
    for head in range(per):
        at = slice(head * size, (head + 1) * size)
        mine[:, at] = jnp.where(core == 0, parts[head], parts[per + head])
        other[:, at] = jnp.where(core == 0, parts[per + head], parts[head])


def attend_back_kernel(
    queries, kv_blocks, logsum, out_grad, score_scale, query_pre, norm_query, cosine, sine, full
):
    heads, rows, size = queries.shape
    width = full.shape[0]
    per = heads // 2
    count = len(kv_blocks)

    def body(*refs):
        q, blocks, refs = refs[0], refs[1 : 1 + count], refs[1 + count :]
        lse, grads, pre, g_query, cos, sin, full = refs[:7]
        kv_grads, (hidden_part, mine, other, gain_grad, kv_acc) = refs[7 : 7 + count], refs[7 + count :]
        core = lax.axis_index("seq")
        query_grads, gains, hidden = [], None, None
        masks = tile_masks(blocks, rows)
        for head in range(heads):
            q_head, g_head = q[head], grads[head]
            low = lse[head]
            probs = [
                jnp.exp(
                    jnp.where(mask, inner_cols(q_head, block[:rows, :size]) * score_scale, NEG)
                    - low
                )
                for block, mask in zip(blocks, masks)
            ]
            prob_grads = [inner_cols(g_head, block[:rows, size:]) for block in blocks]
            weighted = sum(
                (a * b).sum(-1, keepdims=True) for a, b in zip(probs, prob_grads)
            )
            total = None
            for i, (prob, grad, block) in enumerate(zip(probs, prob_grads, blocks)):
                score_grad = (prob * (grad - weighted)).astype(BF)
                part = matmul(score_grad, block[:rows, :size])
                total = part if total is None else total + part
                key_part = inner_rows(score_grad, q_head) * score_scale
                value_part = inner_rows(prob.astype(BF), g_head)
                if head == 0:
                    kv_acc[i, :, :size] = key_part
                    kv_acc[i, :, size:] = value_part
                else:
                    kv_acc[i, :, :size] += key_part
                    kv_acc[i, :, size:] += value_part
            at = slice(head * size, (head + 1) * size)
            back, gain = query_head_back(
                total * score_scale, pre[:, at], g_query[4:5, :], cos[...], sin[...]
            )
            query_grads.append(back)
            gains = gain if gains is None else gains + gain
            part = inner_cols(back, full[:, at])
            hidden = part if hidden is None else hidden + part
        for i in range(count):
            kv_grads[i][...] = kv_acc[i].astype(BF)
        hidden_part[...] = hidden
        split_heads(query_grads, core, mine, other, size)
        gain_grad[...] = gains

    outs = [shape((rows, 2 * size), BF)] * count + [
        shape((rows, width), F32),
        shape((rows, per * size), BF),
        shape((rows, per * size), BF),
        shape((1, size), F32),
    ]
    return kernel_call(
        body,
        outs,
        [
            queries, *kv_blocks, logsum, out_grad, query_pre, norm_query, cosine, sine, full,
        ],
        10 * heads * rows * rows * count * size,
        scratch=[pltpu.VMEM((count, rows, 2 * size), F32)],
        far=tuple(range(2 + count)) + tuple(k + count for k in (3, 5, 6, 7)),
        back=tuple(range(3 + count)),
        room=62,
    )


def gelu_parts(value):
    scale = (2.0 / jnp.pi) ** 0.5
    square = value * value
    tanh = jnp.tanh(scale * (value + 0.044715 * square * value))
    half = 0.5 * (1.0 + tanh)
    slope = half + 0.5 * value * (1.0 - tanh * tanh) * scale * (1.0 + 3 * 0.044715 * square)
    return value * half, slope


def feed_forward(
    inputs, cotangent, context, blocks, unit, wide_gains
):
    heads, rows, size = context.shape
    width = inputs.shape[1]
    half = size // 2
    count = len(blocks)
    hidden = unit * count // 2
    offs = [0, width, 2 * width, 3 * width]
    offs += [offs[3] + hidden, offs[3] + 2 * hidden, offs[3] + 3 * hidden]
    total_cols = offs[6] + heads * half

    def body(x, cot, ctx, *refs):
        blocks, refs = refs[:count], refs[count:]
        gate_at, up_at = slice(0, unit), slice(unit, 2 * unit)
        both_at, down_at, out_at = slice(0, 2 * unit), slice(2 * unit, 3 * unit), slice(3 * unit, None)
        g_attn, g_pre, g_post = [refs[0][k : k + 1, :] for k in (1, 2, 3)]
        result, middle_grad, own, send, ctx_grad, gain_grads = refs[1:7]
        w_out, gate, up, flush = refs[7:]
        place = lax.axis_index("fsdp")
        core = lax.axis_index("seq")
        attn_out = None
        for flip in range(4):
            a, b = blocks[flip][:, out_at], blocks[4 + flip][:, out_at]
            w_out[flip, :, :half] = jnp.where(core == 0, a, b)
            w_out[flip, :, half:] = jnp.where(core == 0, b, a)
            value = ctx[place ^ flip]
            low, high = value[:, :half], value[:, half:]
            at = slice(offs[6] + flip * half, offs[6] + (flip + 1) * half)
            own[:, at] = jnp.where(core == 0, low, high)
            send[:, at] = jnp.where(core == 0, high, low)
            part = inner_cols(value, w_out[flip])
            attn_out = part if attn_out is None else attn_out + part
        inv_attn = rms_scale(attn_out)
        middle = x[...].astype(F32) + attn_out * inv_attn * g_attn
        inv_pre = rms_scale(middle)
        ffn_in = (middle * inv_pre * g_pre).astype(BF)
        own[:, : offs[1]] = ffn_in
        send[:, : offs[1]] = ffn_in
        ffn_out = None
        for i in range(count):
            pre = matmul(ffn_in, blocks[i][:, both_at])
            activated, slope = gelu_parts(pre[:, :unit])
            up_pre = pre[:, unit:]
            gate[i] = up_pre * slope
            up[i] = activated
            mixed = (activated * up_pre).astype(BF)
            j = i % (count // 2)
            dest = own if i < count // 2 else send
            dest[:, offs[3] + j * unit : offs[3] + (j + 1) * unit] = mixed
            part = inner_cols(mixed, blocks[i][:, down_at])
            ffn_out = part if ffn_out is None else ffn_out + part
        inv_post = rms_scale(ffn_out)
        result[...] = middle + ffn_out * inv_post * g_post
        flush(0, slice(0, width))
        for k in (2, 3):
            flush(k, slice(offs[3], offs[4]))
            flush(k, slice(offs[6], total_cols))
        grad = cot[...].astype(F32)
        ffn_grad, post_grad = rms_back(ffn_out, inv_post, g_post, grad)
        ffn_grad = ffn_grad.astype(BF)
        own[:, offs[1] : offs[2]] = ffn_grad
        send[:, offs[1] : offs[2]] = ffn_grad
        pre_total = None
        for i in range(count):
            mixed_grad = matmul(ffn_grad, blocks[i][:, down_at])
            gate_grad = (mixed_grad * gate[i]).astype(BF)
            up_grad = (mixed_grad * up[i]).astype(BF)
            j = i % (count // 2)
            dest = own if i < count // 2 else send
            dest[:, offs[4] + j * unit : offs[4] + (j + 1) * unit] = gate_grad
            dest[:, offs[5] + j * unit : offs[5] + (j + 1) * unit] = up_grad
            part = inner_cols(gate_grad, blocks[i][:, gate_at])
            part = part + inner_cols(up_grad, blocks[i][:, up_at])
            pre_total = part if pre_total is None else pre_total + part
        for k in (2, 3):
            flush(k, slice(offs[4], offs[6]))
            flush(k, slice(0, offs[2]))
        part, pre_grad = rms_back(middle, inv_pre, g_pre, pre_total)
        mid_grad = grad + part
        middle_grad[...] = mid_grad
        attn_grad, attn_gain = rms_back(attn_out, inv_attn, g_attn, mid_grad)
        attn_grad = attn_grad.astype(BF)
        own[:, offs[2] : offs[3]] = attn_grad
        send[:, offs[2] : offs[3]] = attn_grad
        for k in (2, 3):
            flush(k, slice(offs[2], offs[3]))
        for flip in range(4):
            ctx_grad[place ^ flip] = matmul(attn_grad, w_out[flip]).astype(BF)
        gain_grads[...] = jnp.concatenate(
            [attn_gain, pre_grad, post_grad, jnp.zeros((5, width), F32)], 0
        )

    outs = [
        shape((rows, width), F32),
        shape((rows, width), F32),
        shape((rows, total_cols), BF),
        shape((rows, total_cols), BF),
        shape((heads, rows, size), BF),
        shape((8, width), F32),
    ]
    args = [inputs, cotangent, context, *blocks]
    args += [wide_gains]
    scratch = [
        pltpu.VMEM((4, width, size), BF),
        pltpu.VMEM((count, rows, unit), F32),
        pltpu.VMEM((count, rows, unit), F32),
    ]
    flops = 2 * rows * width * (6 * unit * count + 2 * heads * size)
    far = (0, 1) + tuple(range(3, 3 + count))
    back = (0, 1, 2, 3, 5)
    return kernel_call(body, outs, args, flops, scratch, far=far, back=back, room=48, flushes=11), offs


def ffn_weight_grads(own, got, offs, unit, half):
    rows = own.shape[0]
    width = offs[1]

    def body(a, b, *outs):
        def product(left, right):
            return (
                inner_rows(a[:, left], a[:, right]) + inner_rows(b[:, left], b[:, right])
            ).astype(BF)

        at = lambda k, j, size: slice(offs[k] + j * size, offs[k] + (j + 1) * size)
        whole = lambda k: slice(offs[k], offs[k] + width)
        for j, out in enumerate(outs):
            out[:, :unit] = product(whole(0), at(4, j, unit))
            out[:, unit : 2 * unit] = product(whole(0), at(5, j, unit))
            out[:, 2 * unit : 3 * unit] = product(whole(1), at(3, j, unit))
            out[:, 3 * unit :] = product(whole(2), at(6, j, half))

    outs = [shape((width, 3 * unit + half), BF)] * 4
    flops = 4 * rows * width * 4 * (3 * unit + half)
    return kernel_call(body, outs, [own, got], flops, far=(0, 1), back=tuple(range(4)), room=62)


def query_back(query_grad, query_pre, norm_query, cosine, sine, query_full):
    heads, rows, size = query_grad.shape
    width = query_full.shape[0]
    per = heads // 2

    def body(grad, pre, g_query, cos, sin, full, hidden_part, mine, other, gain_grad):
        core = lax.axis_index("seq")
        gains, parts, total = None, [], None
        for head in range(heads):
            at = slice(head * size, (head + 1) * size)
            back, gain = query_head_back(grad[head], pre[:, at], g_query[4:5, :], cos[...], sin[...])
            gains = gain if gains is None else gains + gain
            parts.append(back)
            part = inner_cols(back, full[:, at])
            total = part if total is None else total + part
        hidden_part[...] = total
        split_heads(parts, core, mine, other, size)
        gain_grad[...] = gains

    outs = [
        shape((rows, width), F32),
        shape((rows, per * size), BF),
        shape((rows, per * size), BF),
        shape((1, size), F32),
    ]
    args = [query_grad, query_pre, norm_query, cosine, sine, query_full]
    flops = 2 * rows * width * heads * size
    return kernel_call(body, outs, args, flops, far=(1, 3, 4, 5), back=(0, 1, 2), room=24)


def input_back(
    kv_back, key_pre, norm_key, cosine, sine, kv_full, hidden_part, inputs, norm_in, middle_grad,
    hidden, query_mine, query_other,
):
    rows, width = inputs.shape
    size = norm_key.shape[1]
    per = query_mine.shape[1]
    cols = width + per + size

    def body(
        back, k_pre, g_key, cos, sin, full, part, x, g_in, mid, hid, q_mine, q_other,
        input_grad, own, send, in_gain, key_gain,
    ):
        core = lax.axis_index("seq")
        value = k_pre[...]
        turned = rotate(back[:, :size], cos[...], -sin[...])
        key_grad, gain = rms_back(value, rms_scale(value), g_key[5:6, :], turned)
        key_gain[...] = gain
        key_grad = key_grad.astype(BF)
        value_grad = back[:, size:].astype(BF)
        at = 2 * per
        total = part[...] + inner_cols(key_grad, full[:, at : at + size])
        total = total + inner_cols(value_grad, full[:, at + size :])
        value = x[...].astype(F32)
        grad, gain = rms_back(value, rms_scale(value), g_in[0:1, :], total)
        input_grad[...] = mid[...] + grad
        in_gain[...] = gain
        own[:, :width] = hid[...]
        send[:, :width] = hid[...]
        own[:, width : width + per] = q_mine[...]
        send[:, width : width + per] = q_other[...]
        own[:, width + per :] = jnp.where(core == 0, key_grad, value_grad)
        send[:, width + per :] = jnp.where(core == 0, value_grad, key_grad)

    outs = [
        shape((rows, width), F32),
        shape((rows, cols), BF),
        shape((rows, cols), BF),
        shape((1, width), F32),
        shape((1, size), F32),
    ]
    args = [kv_back, key_pre, norm_key, cosine, sine, kv_full, hidden_part, inputs, norm_in]
    args += [middle_grad, hidden, query_mine, query_other]
    flops = 4 * rows * width * size
    far = (1, 3, 4, 5, 6, 7, 9, 10, 11, 12)
    return kernel_call(body, outs, args, flops, far=far, back=(0, 1, 2), room=24)


def late_grads(own, got, gains, width):
    rows, cols = own.shape
    out_cols = cols - width
    shard = width // 4

    def body(a, b, extra, *refs):
        outs, total = refs[:4], refs[4]
        place = lax.axis_index("fsdp")
        total[...] = inner_rows(a[:, :width], a[:, width:]) + inner_rows(b[:, :width], b[:, width:])
        for flip, out in enumerate(outs):
            out[:shard, :] = total[rows_at((place ^ flip) * shard, shard, 16), :].astype(BF)
            out[shard:, :] = extra[place ^ flip]

    outs = [shape((shard + gains.shape[1], out_cols), BF)] * 4
    flops = 4 * rows * width * out_cols
    scratch = [pltpu.VMEM((width, out_cols), F32)]
    return kernel_call(
        body, outs, [own, got, gains], flops, scratch, far=(0, 1), back=tuple(range(4))
    )


def pick_half(value, which, axis):
    size = value.shape[axis] // 2
    return lax.dynamic_slice_in_dim(value, which * size, size, axis)


def join_cols(mine, other, core):
    return jnp.where(
        core == 0, jnp.concatenate([mine, other], 1), jnp.concatenate([other, mine], 1)
    ).astype(F32)


def after(value, *others):
    return lax.optimization_barrier((value,) + others)[0]


def on_device(ctx_size):
    def run(
        inputs,
        positions,
        block_ids,
        w_query,
        w_key,
        w_value,
        w_out,
        w_gate,
        w_up,
        w_down,
        gain_in,
        gain_query,
        gain_key,
        gain_attn,
        gain_pre,
        gain_post,
        cotangent,
    ):
        core = lax.axis_index("seq")
        fsdp = lax.axis_index("fsdp")
        seq_rows, model_width = inputs.shape[1:]
        head_size = gain_query.shape[0] * 4
        half_rows = seq_rows // 2
        score_scale = head_size ** (-0.5)
        inputs, cotangent = inputs[0], cotangent[0]

        gains = [gain_in, gain_attn, gain_pre, gain_post, gain_query, gain_key]
        gain_sizes = [member.shape[0] for member in gains]
        shard_rows = w_key.shape[0]
        packed, packed_other = pack(w_query, w_key, w_value, gains)
        first = [packed] + [swap(packed, "fsdp", flip, 4) for flip in (1, 2, 3)]
        first_other = [packed_other] + [swap_pair(block) for block in first[1:]]
        (ffn_mine, ffn_other), unit = pack_ffn(w_gate, w_up, w_down, w_out)
        sent = after(ffn_mine, *first[1:])
        ffn_one = swap(sent, "fsdp", 1, 4)
        ffn_two = swap(sent, "fsdp", 2, 4)

        cosine, sine = tables(positions[0], head_size)
        hidden, key_pre, packed_kv, query_pre, queries, qkv_full, wide_gains, narrow_gains = project(
            inputs, first, first_other, head_size, cosine, sine, block_ids
        )
        if ctx_size == 4:
            kv_one, kv_two = swap(packed_kv, "ctx", 1, 4), swap(packed_kv, "ctx", 3, 4)
            sent = jnp.where(core == 0, kv_one, kv_two)
            ffn_one, ffn_two, sent = lax.optimization_barrier((ffn_one, ffn_two, sent))
            kv_blocks = [packed_kv, kv_one, kv_two, swap_split(sent, "ctx", 4, 3, 1)]
        else:
            kv_all = lax.all_gather(packed_kv, "ctx", axis=0)
        if ctx_size == 4:
            context, logsum = attend_kernel(queries, kv_blocks, score_scale)
        else:
            offsets = jnp.arange(half_rows, dtype=jnp.int32)
            block_all = kv_all[:, seq_rows : seq_rows + 2, 0].astype(jnp.int32)
            key_order = (block_all[:, :, None] * half_rows + offsets).reshape(-1)
            query_order = (block_ids[0][:, None] * half_rows + offsets).reshape(-1)
            key_all = kv_all[:, :seq_rows, :head_size].reshape(-1, head_size)
            value_all = kv_all[:, :seq_rows, head_size:].reshape(-1, head_size)
            by_row = queries.transpose(1, 0, 2)
            seq_out, logsum = attend_forward(
                by_row, key_all, value_all, query_order, key_order, score_scale
            )
            context = seq_out.astype(BF).transpose(1, 0, 2)

        ffn_opposite = swap_split(jnp.where(core == 0, ffn_one, ffn_two), "fsdp", 4, 2, 1)
        ffn_blocks = [ffn_mine, ffn_one, ffn_two, after(ffn_opposite, context)]
        ffn_blocks += [ffn_other] + [swap_pair(block) for block in ffn_blocks[1:]]

        (result, middle_grad, own, send, context_grad, gain_grads), offs = feed_forward(
            inputs,
            cotangent,
            context,
            ffn_blocks,
            unit,
            wide_gains,
        )

        parts = ffn_weight_grads(own, swap_pair(send), offs, unit, head_size // 2)
        order = Order()
        ffn_steps = reduce_steps(parts, core, ctx_size, (2 * unit,), order)
        next(ffn_steps)
        context_grad = after(context_grad, parts[0])

        if ctx_size == 4:
            *kv_parts, hidden_part, back_mine, back_other, grad_query = attend_back_kernel(
                queries,
                kv_blocks,
                logsum,
                context_grad,
                score_scale,
                query_pre,
                narrow_gains,
                cosine,
                sine,
                qkv_full,
            )
            kv_via = swap_split(kv_parts[3], "ctx", 4, 3, 1)
        else:
            query_grad, key_grad, value_grad = attend_backward(
                by_row,
                key_all,
                value_all,
                query_order,
                key_order,
                score_scale,
                logsum,
                context_grad.transpose(1, 0, 2),
            )
            query_grad = query_grad.transpose(1, 0, 2)
            kv_grad = jnp.concatenate([key_grad, value_grad], 1).astype(BF)
            hidden_part, back_mine, back_other, grad_query = query_back(
                query_grad, query_pre, narrow_gains, cosine, sine, qkv_full
            )
            kv_back = lax.psum_scatter(kv_grad, "ctx", scatter_dimension=0, tiled=True).astype(F32)
        next(ffn_steps)
        if ctx_size == 4:
            kv_back = scatter4(kv_parts, order.wait(kv_via), core, "ctx", 4, 1, 3, order)
        kv_back = order.wait(kv_back)
        input_grad, own, send, grad_in, grad_key = input_back(
            kv_back,
            key_pre,
            narrow_gains,
            cosine,
            sine,
            qkv_full,
            hidden_part,
            inputs,
            wide_gains,
            middle_grad,
            hidden,
            back_mine,
            back_other,
        )
        gain_list = (grad_in, gain_grads[0], gain_grads[1], gain_grads[2], grad_query, grad_key)
        gain_rows = jnp.concatenate([member.reshape(4, 1, -1) for member in gain_list], 2)
        width = own.shape[1] - model_width
        gain_count = -(-gain_rows.shape[2] // width)
        gain_rows = jnp.pad(gain_rows, ((0, 0), (0, 0), (0, gain_count * width - gain_rows.shape[2])))
        gain_rows = gain_rows.reshape(4, gain_count, width).astype(BF)
        gain_rows = jnp.pad(gain_rows, ((0, 0), (0, 32 - gain_count), (0, 0)))
        late_parts = late_grads(own, swap_pair(send), gain_rows, model_width)
        late_steps = reduce_steps(late_parts, core, ctx_size, (), order)
        chains = {"f": ffn_steps, "l": late_steps}
        results = {}
        turns = "lf"
        while len(results) < 2:
            for name in turns:
                if name not in results:
                    got = next(chains[name])
                    if got is not None:
                        results[name] = got
        (gu_sum, rest_sum), (gu_other, rest_other) = results["f"]
        (late_sum,), (late_other,) = results["l"]
        rest_sum, rest_other = rest_sum.T, rest_other.T
        total_down = join(rest_sum[:unit], rest_other[:unit], core).astype(F32)
        total_out = join(rest_sum[unit:], rest_other[unit:], core).astype(F32)
        total_gate = join_cols(gu_sum[:, :unit], gu_other[:, :unit], core)
        total_up = join_cols(gu_sum[:, unit:], gu_other[:, unit:], core)

        query_cols = width - head_size
        total_query = join_cols(
            late_sum[:shard_rows, :query_cols], late_other[:shard_rows, :query_cols], core
        )
        total_key = jnp.where(core == 0, late_sum, late_other)[:shard_rows, query_cols:].astype(F32)
        total_value = jnp.where(core == 0, late_other, late_sum)[:shard_rows, query_cols:].astype(F32)
        gain_at = slice(shard_rows, shard_rows + gain_count)
        gain_total = (late_sum[gain_at].astype(F32) + late_other[gain_at].astype(F32)).reshape(-1)
        outs = []
        start = 0
        for size in gain_sizes:
            outs.append(gain_total[start : start + size])
            start += size
        g_in, g_attn, g_pre, g_post, g_query, g_key = outs
        return (
            result[None],
            input_grad[None],
            total_query,
            total_key,
            total_value,
            total_out,
            total_gate,
            total_up,
            total_down,
            g_in,
            g_query,
            g_key,
            g_attn,
            g_pre,
            g_post,
        )

    return run


def solution(mesh):
    rows = P(("seq", "fsdp"), "ctx")
    wide = P(("seq", "fsdp"), "ctx", None)
    first = P("fsdp", None)
    second = P(None, "fsdp")
    flat = P("fsdp")
    in_specs = (wide, rows, rows, first, first, first, first, second, second, first)
    in_specs += (flat,) * 6 + (wide,)
    out_specs = (wide, wide, first, first, first, first, second, second, first) + (flat,) * 6
    return jax.shard_map(
        on_device(mesh.shape["ctx"]),
        mesh=mesh,
        in_specs=in_specs,
        out_specs=out_specs,
        check_vma=False,
    )
```

```python
import jax
import jax.numpy as jnp
from jax import lax
from jax.experimental import pallas as pl
from jax.experimental.pallas import tpu as pltpu
from jax.sharding import PartitionSpec as P

EPS = 1e-06
THETA = 1000000.0
NEG = -1e30
BF = jnp.bfloat16
F32 = jnp.float32


def matmul(left, right):
    return jnp.dot(left, right, preferred_element_type=F32)


def inner_cols(left, right):
    return lax.dot_general(left, right, (((1,), (1,)), ((), ())), preferred_element_type=F32)


def inner_rows(left, right):
    return lax.dot_general(left, right, (((0,), (0,)), ((), ())), preferred_element_type=F32)


def rotate(value, cosine, sine_table):
    half = value.shape[-1] // 2
    first = value[..., :half]
    second = value[..., half:]
    return jnp.concatenate(
        [first * cosine - second * sine_table, second * cosine + first * sine_table], axis=-1
    )


def tables(positions, head_size):
    half = head_size // 2
    freq = 1.0 / THETA ** (jnp.arange(half, dtype=F32) * 2.0 / head_size)
    angle = positions.astype(F32)[:, None] * freq[None, :]
    return (jnp.cos(angle), jnp.sin(angle))


def swap(value, axis, flip, size):
    return lax.ppermute(value, axis, [(i, i ^ flip) for i in range(size)])


def swap_pair(value):
    return swap(value, "seq", 1, 2)


def swap_split(value, axis, size, flip0, flip1):
    perm = [(i, i ^ flip0) for i in range(size)]
    perm += [(size + i, size + (i ^ flip1)) for i in range(size)]
    return lax.ppermute(value, ("seq", axis), perm)


def by_core(core, one, two):
    return jnp.where(core == 0, one, two), jnp.where(core == 0, two, one)


def scatter4(blocks, axis, size, first, second, order, at_once=False):
    own, passing, both = blocks
    both = swap_split(both if at_once else order(both), axis, size, second, first)
    yield
    both = order.wait(both)
    passing = (passing.astype(F32) + both[1].astype(F32)).astype(BF)
    passing = swap_split(order(passing), axis, size, first, second)
    yield
    yield own.astype(F32) + order.wait(passing).astype(F32) + both[0].astype(F32)


def halves(value, pick):
    axis = value.ndim - 2
    rows = value.shape[axis] // 2
    keep = lax.dynamic_slice_in_dim(value, pick * rows, rows, axis)
    send = lax.dynamic_slice_in_dim(value, (1 - pick) * rows, rows, axis)
    return keep, send


def join(mine, other, pick):
    return jnp.where(
        pick == 0, jnp.concatenate([mine, other], 0), jnp.concatenate([other, mine], 0)
    )


class Order:
    def __init__(self):
        self.last = None

    def __call__(self, value):
        if self.last is not None:
            value = lax.optimization_barrier((value, self.last))[0]
        self.last = value
        return value

    def wait(self, value):
        return lax.optimization_barrier((value, self.last))[0]


def reduce_steps(blocks, ctx_size, cuts, order):
    place = lax.axis_index("ctx")
    high = place // 2
    odd = lax.rem(place, 2)
    mixed = lax.rem(high + odd, 2)
    steps = [(1, mixed), (3, high)]
    for value in scatter4(blocks, "fsdp", 4, 1, 2, order):
        if value is None:
            yield
    if ctx_size != 4:
        value = lax.psum(value.astype(BF), "ctx")
    elif not cuts:
        for flip in (1, 3):
            value = value.astype(BF)
            got = swap(order(value), "ctx", flip, 4)
            yield
            value = value.astype(F32) + order.wait(got).astype(F32)
        value = value.astype(BF)
    pieces = [value]
    if cuts:
        edges = [0, *cuts, value.shape[1]]
        pieces = [value[:, a:b] for a, b in zip(edges, edges[1:])]
    if cuts and ctx_size == 4:
        turns = [steps, steps[::-1]]
        for k in range(2):
            got, keep = [], []
            for piece, turn in zip(pieces, turns):
                flip, pick = turn[k]
                kept, send = halves(piece, pick)
                keep.append(kept)
                got.append(swap(order(send.astype(BF)), "ctx", flip, 4))
            yield
            pieces = [a.astype(F32) + order.wait(b).astype(F32) for a, b in zip(keep, got)]
        pieces = [piece.astype(BF) for piece in pieces]
        for k in (1, 0):
            got = [swap(order(p), "ctx", turn[k][0], 4) for p, turn in zip(pieces, turns)]
            yield
            pieces = [
                join(p, order.wait(b), turn[k][1]) for p, b, turn in zip(pieces, got, turns)
            ]
    others = [swap_pair(order(piece)) for piece in pieces]
    yield
    yield pieces, others


def attend_forward(queries, key_rows, values, query_order, key_order, score_scale):
    allowed = key_order[None, :] <= query_order[:, None]
    outputs = []
    logsums = []
    for head_index in range(queries.shape[1]):
        scores = inner_cols(queries[:, head_index], key_rows) * score_scale
        scores = jnp.where(allowed, scores, NEG)
        highest = jnp.max(scores, axis=-1, keepdims=True)
        weights = jnp.exp(scores - highest)
        summed = jnp.sum(weights, axis=-1, keepdims=True)
        probs = (weights / summed).astype(BF)
        outputs.append(matmul(probs, values))
        logsums.append(highest + jnp.log(summed))
    return (jnp.stack(outputs, axis=1), jnp.stack(logsums, axis=1))


def attend_backward(
    queries, key_rows, values, query_order, key_order, score_scale, logsums, out_grad
):
    allowed = key_order[None, :] <= query_order[:, None]
    query_grads = []
    key_grad = jnp.zeros(key_rows.shape, F32)
    value_grad = jnp.zeros(values.shape, F32)
    for head_index in range(queries.shape[1]):
        query_head = queries[:, head_index]
        grad_head = out_grad[:, head_index]
        scores = inner_cols(query_head, key_rows) * score_scale
        scores = jnp.where(allowed, scores, NEG)
        probs = jnp.exp(scores - logsums[:, head_index])
        value_grad = value_grad + inner_rows(probs.astype(BF), grad_head)
        prob_grad = inner_cols(grad_head, values)
        weighted = jnp.sum(probs * prob_grad, axis=-1, keepdims=True)
        score_grad = (probs * (prob_grad - weighted)).astype(BF)
        query_grads.append(matmul(score_grad, key_rows) * score_scale)
        key_grad = key_grad + inner_rows(score_grad, query_head) * score_scale
    return (jnp.stack(query_grads, axis=1), key_grad, value_grad)


class Waiting:
    def __init__(self, ref, copy):
        self.ref, self.copy = ref, copy

    def wait(self):
        if self.copy is not None:
            self.copy.wait()
            self.copy = None

    def __getitem__(self, index):
        self.wait()
        return self.ref[index]


def kernel_call(body, outs, args, flops, scratch=(), smem=(), far=(), back=(), room=16, flushes=0):
    nbytes = sum(a.size * a.dtype.itemsize for a in args)
    nbytes += sum(o.size * o.dtype.itemsize for o in outs)
    hbm = pl.BlockSpec(memory_space=pltpu.HBM)
    specs = {i: hbm for i in far}
    specs.update({i: pl.BlockSpec(memory_space=pltpu.SMEM) for i in smem})
    n_in, n_out, n_own = len(args), len(outs), len(scratch)

    def wrapped(*refs):
        ins, dests = list(refs[:n_in]), list(refs[n_in : n_in + n_out])
        rest = refs[n_in + n_out :]
        own, rest = rest[:n_own], rest[n_own:]
        sems = rest[-1]
        for k, i in enumerate(far):
            copy = pltpu.make_async_copy(ins[i], rest[k], sems.at[k])
            copy.start()
            ins[i] = Waiting(rest[k], copy)
        kept = list(dests)
        for k, i in enumerate(back):
            kept[i] = rest[len(far) + k]
        copies = []
        flushed = set()

        def flush(which, cols):
            at = (slice(None), cols)
            sem = sems.at[len(far) + len(back) + len(copies)]
            copies.append(pltpu.make_async_copy(kept[which].at[at], dests[which].at[at], sem))
            copies[-1].start()
            flushed.add(which)

        body(*ins, *kept, *own, *([flush] if flushes else []))
        for k, i in enumerate(back):
            if i in flushed:
                continue
            copies.append(pltpu.make_async_copy(kept[i], dests[i], sems.at[len(far) + k]))
            copies[-1].start()
        for i in far:
            ins[i].wait()
        for copy in copies:
            copy.wait()

    buffers = [pltpu.VMEM(args[i].shape, args[i].dtype) for i in far]
    buffers += [pltpu.VMEM(outs[i].shape, outs[i].dtype) for i in back]
    return pl.pallas_call(
        wrapped,
        out_shape=outs,
        in_specs=[specs.get(i, pl.BlockSpec()) for i in range(n_in)],
        out_specs=[hbm if i in back else pl.BlockSpec() for i in range(n_out)],
        scratch_shapes=list(scratch)
        + buffers
        + [pltpu.SemaphoreType.DMA((max(1, len(far) + len(back) + flushes),))],
        compiler_params=pltpu.CompilerParams(vmem_limit_bytes=room * 1024 * 1024),
        cost_estimate=pl.CostEstimate(flops=flops, bytes_accessed=nbytes, transcendentals=0),
    )(*args)


def shape(dims, kind):
    return jax.ShapeDtypeStruct(dims, kind)


def rms_scale(value):
    return lax.rsqrt(jnp.mean(value * value, axis=-1, keepdims=True) + EPS)


def rms_back(value, inverse, gain, grad):
    scaled = value * inverse
    gain_grad = jnp.sum(grad * scaled, axis=0, keepdims=True)
    weighted = grad * gain
    mean = jnp.mean(weighted * scaled, axis=-1, keepdims=True)
    return inverse * (weighted - scaled * mean), gain_grad


def rows_at(start, size, step):
    return pl.ds(pl.multiple_of(start, step), size)


def pack(w_query, w_key, w_value, gains):
    rows = w_query.shape[0] // 2
    widths = [w.shape[1] for w in (w_query, w_key, w_value)]
    total = sum(widths)

    def body(*refs):
        weights, (mine, other) = refs[:3], refs[-2:]
        core = lax.axis_index("seq")
        start = 0
        for ref, width in zip(weights, widths):
            at = slice(start, start + width)
            low, high = ref[:rows, :], ref[rows:, :]
            mine[:rows, at] = jnp.where(core == 0, low, high)
            other[:, at] = jnp.where(core == 0, high, low)
            start += width
        mine[rows:, :] = jnp.zeros((16, total), BF)
        for number, (ref, gain) in enumerate(zip(refs[3:-2], gains)):
            row = ref[...].astype(F32).reshape(1, gain.shape[0])
            mine[rows + number : rows + number + 1, : gain.shape[0]] = row.astype(BF)

    outs = [shape((rows + 16, total), BF), shape((rows, total), BF)]
    args = [w_query, w_key, w_value, *gains]
    return kernel_call(body, outs, args, 0, room=62)


def pack_ffn(w_gate, w_up, w_down, w_out):
    width = w_gate.shape[0]
    sizes = [w_gate.shape[1] // 2, w_up.shape[1] // 2, w_down.shape[0] // 2, w_out.shape[0] // 2]
    total = sum(sizes)

    def body(gate, up, down, out, mine, other):
        core = lax.axis_index("seq")
        start = 0
        for ref, size, turn in zip((gate, up, down, out), sizes, (False, False, True, True)):
            at = slice(start, start + size)
            low = ref[:size, :].T if turn else ref[:, :size]
            high = ref[size:, :].T if turn else ref[:, size:]
            mine[:, at] = jnp.where(core == 0, low, high)
            other[:, at] = jnp.where(core == 0, high, low)
            start += size

    outs = [shape((width, total), BF)] * 2
    args = [w_gate, w_up, w_down, w_out]
    return kernel_call(body, outs, args, 0, room=62), sizes[0]


def project(inputs, mine, other, size, cosine, sine, block_ids):
    rows, width = inputs.shape
    part, total = other[0].shape
    cols = total - 2 * size
    heads = cols // size

    def body(x, *refs):
        blocks, refs = refs[:8], refs[8:]
        cos, sin, ids = refs[:3]
        hidden, key_pre, packed, query_pre, queries, full, wide, narrow = refs[3:]
        place = lax.axis_index("fsdp")
        core = lax.axis_index("seq")
        for flip in range(4):
            start = (place ^ flip) * 2
            full[rows_at((start + core) * part, part, 16), :] = blocks[flip][:part, :]
            full[rows_at((start + 1 - core) * part, part, 16), :] = blocks[4 + flip][:part, :]
        rows_of = [blocks[flip][part:, : width // 4].astype(F32) for flip in range(4)]
        for index in range(4):
            piece = rows_of[0]
            for flip in range(1, 4):
                piece = jnp.where((place ^ flip) == index, rows_of[flip], piece)
            wide[:, index * (width // 4) : (index + 1) * (width // 4)] = piece
            narrow[:, index * (size // 4) : (index + 1) * (size // 4)] = piece[:, : size // 4]
        g_in, g_query, g_key = wide[0:1, :], narrow[4:5, :], narrow[5:6, :]
        value = x[...].astype(F32)
        hid = (value * rms_scale(value) * g_in).astype(BF)
        hidden[...] = hid
        both = matmul(hid, full[:, cols:])
        key = both[:, :size]
        key_pre[...] = key
        turned = rotate(key * rms_scale(key) * g_key, cos[...], sin[...])
        packed[:rows, :size] = turned.astype(BF)
        packed[:rows, size:] = both[:, size:].astype(BF)
        row = lax.broadcasted_iota(jnp.int32, (16, 2 * size), 0)
        packed[rows:, :] = jnp.where(row == 0, ids[0, 0], ids[0, 1]).astype(F32).astype(BF)
        for head in range(heads):
            at = slice(head * size, (head + 1) * size)
            value = matmul(hid, full[:, at])
            query_pre[:, at] = value
            turned = rotate(value * rms_scale(value) * g_query, cos[...], sin[...])
            queries[head] = turned.astype(BF)

    outs = [
        shape((rows, width), BF),
        shape((rows, size), F32),
        shape((rows + 16, 2 * size), BF),
        shape((rows, cols), F32),
        shape((heads, rows, size), BF),
        shape((width, total), BF),
        shape((16, width), F32),
        shape((16, size), F32),
    ]
    args = [inputs, *mine, *other, cosine, sine, block_ids]
    flops = 2 * rows * width * total
    far = (0, 9, 10)
    return kernel_call(body, outs, args, flops, smem=(11,), far=far, back=(0, 1, 3, 5), room=62)


def tile_masks(blocks, rows):
    half = rows // 2
    lane = lax.broadcasted_iota(jnp.int32, (1, half), 1).astype(F32)
    row = lax.broadcasted_iota(jnp.int32, (rows, 1), 0)
    own = blocks[0][rows : rows + 16, :half].astype(F32)
    low, high = own[0:1, 0:1], own[1:2, 0:1]
    query_order = jnp.where(row < half, low, high) * half
    query_order = query_order + jnp.where(row < half, row, row - half).astype(F32)
    masks = []
    for block in blocks:
        ids = block[rows : rows + 16, :half].astype(F32)
        keys = jnp.concatenate([ids[0:1] * half + lane, ids[1:2] * half + lane], 1)
        masks.append(keys <= query_order)
    return masks


def attend_kernel(queries, kv_blocks, score_scale):
    heads, rows, size = queries.shape
    count = len(kv_blocks)

    def body(*refs):
        q, blocks, (context, logsum) = refs[0], refs[1 : 1 + count], refs[1 + count :]
        masks = tile_masks(blocks, rows)
        for head in range(heads):
            scores = [
                jnp.where(mask, inner_cols(q[head], block[:rows, :size]) * score_scale, NEG)
                for block, mask in zip(blocks, masks)
            ]
            highest = scores[0].max(-1, keepdims=True)
            for tile in scores[1:]:
                highest = jnp.maximum(highest, tile.max(-1, keepdims=True))
            weights = [jnp.exp(tile - highest) for tile in scores]
            summed = sum(tile.sum(-1, keepdims=True) for tile in weights)
            inverse = 1.0 / summed
            out = sum(
                matmul((tile * inverse).astype(BF), block[:rows, size:])
                for tile, block in zip(weights, blocks)
            )
            context[head] = out.astype(BF)
            logsum[head] = highest + jnp.log(summed)

    outs = [shape((heads, rows, size), BF), shape((heads, rows, 1), F32)]
    flops = 4 * heads * rows * rows * count * size
    far = tuple(range(1, 1 + count))
    return kernel_call(body, outs, [queries, *kv_blocks], flops, far=far, room=24)


def query_head_back(grad, value, gain, cosine, sine):
    turned = rotate(grad, cosine, -sine)
    back, gain_grad = rms_back(value, rms_scale(value), gain, turned)
    return back.astype(BF), gain_grad


def split_heads(parts, core, mine, other, size):
    per = len(parts) // 2
    for head in range(per):
        at = slice(head * size, (head + 1) * size)
        mine[:, at] = jnp.where(core == 0, parts[head], parts[per + head])
        other[:, at] = jnp.where(core == 0, parts[per + head], parts[head])


def attend_back_kernel(
    queries, kv_blocks, logsum, out_grad, score_scale, query_pre, norm_query, cosine, sine, full
):
    heads, rows, size = queries.shape
    width = full.shape[0]
    per = heads // 2
    count = len(kv_blocks)

    def body(*refs):
        q, blocks, refs = refs[0], refs[1 : 1 + count], refs[1 + count :]
        lse, grads, pre, g_query, cos, sin, full = refs[:7]
        kv_grads, (hidden_part, mine, other, gain_grad, kv_acc) = refs[7:10], refs[10:]
        core = lax.axis_index("seq")
        query_grads, gains, hidden = [], None, None
        masks = tile_masks(blocks, rows)
        for head in range(heads):
            q_head, g_head = q[head], grads[head]
            low = lse[head]
            probs = [
                jnp.exp(
                    jnp.where(mask, inner_cols(q_head, block[:rows, :size]) * score_scale, NEG)
                    - low
                )
                for block, mask in zip(blocks, masks)
            ]
            prob_grads = [inner_cols(g_head, block[:rows, size:]) for block in blocks]
            weighted = sum(
                (a * b).sum(-1, keepdims=True) for a, b in zip(probs, prob_grads)
            )
            total = None
            for i, (prob, grad, block) in enumerate(zip(probs, prob_grads, blocks)):
                score_grad = (prob * (grad - weighted)).astype(BF)
                part = matmul(score_grad, block[:rows, :size])
                total = part if total is None else total + part
                key_part = inner_rows(score_grad, q_head) * score_scale
                value_part = inner_rows(prob.astype(BF), g_head)
                if head == 0:
                    kv_acc[i, :, :size] = key_part
                    kv_acc[i, :, size:] = value_part
                else:
                    kv_acc[i, :, :size] += key_part
                    kv_acc[i, :, size:] += value_part
            at = slice(head * size, (head + 1) * size)
            back, gain = query_head_back(
                total * score_scale, pre[:, at], g_query[4:5, :], cos[...], sin[...]
            )
            query_grads.append(back)
            gains = gain if gains is None else gains + gain
            part = inner_cols(back, full[:, at])
            hidden = part if hidden is None else hidden + part
        one, two = by_core(core, kv_acc[1], kv_acc[2])
        kv_grads[0][...] = kv_acc[0].astype(BF)
        kv_grads[1][...] = one.astype(BF)
        kv_grads[2][0] = two.astype(BF)
        kv_grads[2][1] = kv_acc[3].astype(BF)
        hidden_part[...] = hidden
        split_heads(query_grads, core, mine, other, size)
        gain_grad[...] = gains

    block = (rows, 2 * size)
    outs = [shape(block, BF), shape(block, BF), shape((2, *block), BF)] + [
        shape((rows, width), F32),
        shape((rows, per * size), BF),
        shape((rows, per * size), BF),
        shape((1, size), F32),
    ]
    return kernel_call(
        body,
        outs,
        [
            queries, *kv_blocks, logsum, out_grad, query_pre, norm_query, cosine, sine, full,
        ],
        10 * heads * rows * rows * count * size,
        scratch=[pltpu.VMEM((count, rows, 2 * size), F32)],
        far=tuple(range(2 + count)) + tuple(k + count for k in (3, 5, 6, 7)),
        back=tuple(range(6)),
        room=62,
    )


def gelu_parts(value):
    scale = (2.0 / jnp.pi) ** 0.5
    square = value * value
    tanh = jnp.tanh(scale * (value + 0.044715 * square * value))
    half = 0.5 * (1.0 + tanh)
    slope = half + 0.5 * value * (1.0 - tanh * tanh) * scale * (1.0 + 3 * 0.044715 * square)
    return value * half, slope


def feed_forward(
    inputs, cotangent, context, blocks, unit, wide_gains
):
    heads, rows, size = context.shape
    width = inputs.shape[1]
    half = size // 2
    count = len(blocks)
    hidden = unit * count // 2
    offs = [0, width, 2 * width, 3 * width]
    offs += [offs[3] + hidden, offs[3] + 2 * hidden, offs[3] + 3 * hidden]
    total_cols = offs[6] + heads * half

    def body(x, cot, ctx, *refs):
        blocks, refs = refs[:count], refs[count:]
        gate_at, up_at = slice(0, unit), slice(unit, 2 * unit)
        both_at, down_at, out_at = slice(0, 2 * unit), slice(2 * unit, 3 * unit), slice(3 * unit, None)
        g_attn, g_pre, g_post = [refs[0][k : k + 1, :] for k in (1, 2, 3)]
        result, middle_grad, own, send, ctx_grad, gain_grads = refs[1:7]
        w_out, gate, up, flush = refs[7:]
        place = lax.axis_index("fsdp")
        core = lax.axis_index("seq")
        attn_out = None
        for flip in range(4):
            a, b = blocks[flip][:, out_at], blocks[4 + flip][:, out_at]
            w_out[flip, :, :half] = jnp.where(core == 0, a, b)
            w_out[flip, :, half:] = jnp.where(core == 0, b, a)
            value = ctx[place ^ flip]
            low, high = value[:, :half], value[:, half:]
            at = slice(offs[6] + flip * half, offs[6] + (flip + 1) * half)
            own[:, at] = jnp.where(core == 0, low, high)
            send[:, at] = jnp.where(core == 0, high, low)
            part = inner_cols(value, w_out[flip])
            attn_out = part if attn_out is None else attn_out + part
        inv_attn = rms_scale(attn_out)
        middle = x[...].astype(F32) + attn_out * inv_attn * g_attn
        inv_pre = rms_scale(middle)
        ffn_in = (middle * inv_pre * g_pre).astype(BF)
        own[:, : offs[1]] = ffn_in
        send[:, : offs[1]] = ffn_in
        ffn_out = None
        for i in range(count):
            pre = matmul(ffn_in, blocks[i][:, both_at])
            activated, slope = gelu_parts(pre[:, :unit])
            up_pre = pre[:, unit:]
            gate[i] = up_pre * slope
            up[i] = activated
            mixed = (activated * up_pre).astype(BF)
            j = i % (count // 2)
            dest = own if i < count // 2 else send
            dest[:, offs[3] + j * unit : offs[3] + (j + 1) * unit] = mixed
            part = inner_cols(mixed, blocks[i][:, down_at])
            ffn_out = part if ffn_out is None else ffn_out + part
        inv_post = rms_scale(ffn_out)
        result[...] = middle + ffn_out * inv_post * g_post
        flush(0, slice(0, width))
        for k in (2, 3):
            flush(k, slice(offs[3], offs[4]))
            flush(k, slice(offs[6], total_cols))
        grad = cot[...].astype(F32)
        ffn_grad, post_grad = rms_back(ffn_out, inv_post, g_post, grad)
        ffn_grad = ffn_grad.astype(BF)
        own[:, offs[1] : offs[2]] = ffn_grad
        send[:, offs[1] : offs[2]] = ffn_grad
        pre_total = None
        for i in range(count):
            mixed_grad = matmul(ffn_grad, blocks[i][:, down_at])
            gate_grad = (mixed_grad * gate[i]).astype(BF)
            up_grad = (mixed_grad * up[i]).astype(BF)
            j = i % (count // 2)
            dest = own if i < count // 2 else send
            dest[:, offs[4] + j * unit : offs[4] + (j + 1) * unit] = gate_grad
            dest[:, offs[5] + j * unit : offs[5] + (j + 1) * unit] = up_grad
            part = inner_cols(gate_grad, blocks[i][:, gate_at])
            part = part + inner_cols(up_grad, blocks[i][:, up_at])
            pre_total = part if pre_total is None else pre_total + part
        for k in (2, 3):
            flush(k, slice(offs[4], offs[6]))
            flush(k, slice(0, offs[2]))
        part, pre_grad = rms_back(middle, inv_pre, g_pre, pre_total)
        mid_grad = grad + part
        middle_grad[...] = mid_grad
        attn_grad, attn_gain = rms_back(attn_out, inv_attn, g_attn, mid_grad)
        attn_grad = attn_grad.astype(BF)
        own[:, offs[2] : offs[3]] = attn_grad
        send[:, offs[2] : offs[3]] = attn_grad
        for k in (2, 3):
            flush(k, slice(offs[2], offs[3]))
        for flip in range(4):
            ctx_grad[place ^ flip] = matmul(attn_grad, w_out[flip]).astype(BF)
        gain_grads[...] = jnp.concatenate(
            [attn_gain, pre_grad, post_grad, jnp.zeros((5, width), F32)], 0
        )

    outs = [
        shape((rows, width), F32),
        shape((rows, width), F32),
        shape((rows, total_cols), BF),
        shape((rows, total_cols), BF),
        shape((heads, rows, size), BF),
        shape((8, width), F32),
    ]
    args = [inputs, cotangent, context, *blocks]
    args += [wide_gains]
    scratch = [
        pltpu.VMEM((4, width, size), BF),
        pltpu.VMEM((count, rows, unit), F32),
        pltpu.VMEM((count, rows, unit), F32),
    ]
    flops = 2 * rows * width * (6 * unit * count + 2 * heads * size)
    far = (0, 1) + tuple(range(3, 3 + count))
    back = (0, 1, 2, 3, 5)
    return kernel_call(body, outs, args, flops, scratch, far=far, back=back, room=48, flushes=11), offs


def ffn_weight_grads(own, got, offs, unit, half):
    rows = own.shape[0]
    width = offs[1]

    def body(a, b, *outs):
        def product(left, right):
            return (
                inner_rows(a[:, left], a[:, right]) + inner_rows(b[:, left], b[:, right])
            ).astype(BF)

        at = lambda k, j, size: slice(offs[k] + j * size, offs[k] + (j + 1) * size)
        whole = lambda k: slice(offs[k], offs[k] + width)
        core = lax.axis_index("seq")
        for left, k, size, start in ((0, 4, unit, 0), (0, 5, unit, 1), (1, 3, unit, 2), (2, 6, half, 3)):
            cols = slice(start * unit, start * unit + size)
            own, one, two, far = [product(whole(left), at(k, j, size)) for j in range(4)]
            one, two = by_core(core, one, two)
            outs[0][:, cols] = own
            outs[1][:, cols] = one
            outs[2][0, :, cols] = two
            outs[2][1, :, cols] = far

    block = (width, 3 * unit + half)
    outs = [shape(block, BF), shape(block, BF), shape((2, *block), BF)]
    flops = 4 * rows * width * 4 * (3 * unit + half)
    return kernel_call(body, outs, [own, got], flops, far=(0, 1), back=(0, 1, 2), room=62)


def query_back(query_grad, query_pre, norm_query, cosine, sine, query_full):
    heads, rows, size = query_grad.shape
    width = query_full.shape[0]
    per = heads // 2

    def body(grad, pre, g_query, cos, sin, full, hidden_part, mine, other, gain_grad):
        core = lax.axis_index("seq")
        gains, parts, total = None, [], None
        for head in range(heads):
            at = slice(head * size, (head + 1) * size)
            back, gain = query_head_back(grad[head], pre[:, at], g_query[4:5, :], cos[...], sin[...])
            gains = gain if gains is None else gains + gain
            parts.append(back)
            part = inner_cols(back, full[:, at])
            total = part if total is None else total + part
        hidden_part[...] = total
        split_heads(parts, core, mine, other, size)
        gain_grad[...] = gains

    outs = [
        shape((rows, width), F32),
        shape((rows, per * size), BF),
        shape((rows, per * size), BF),
        shape((1, size), F32),
    ]
    args = [query_grad, query_pre, norm_query, cosine, sine, query_full]
    flops = 2 * rows * width * heads * size
    return kernel_call(body, outs, args, flops, far=(1, 3, 4, 5), back=(0, 1, 2), room=24)


def input_back(
    kv_back, key_pre, norm_key, cosine, sine, kv_full, hidden_part, inputs, norm_in, middle_grad,
    hidden, query_mine, query_other,
):
    rows, width = inputs.shape
    size = norm_key.shape[1]
    per = query_mine.shape[1]
    cols = width + per + size

    def body(
        back, k_pre, g_key, cos, sin, full, part, x, g_in, mid, hid, q_mine, q_other,
        input_grad, own, send, in_gain, key_gain,
    ):
        core = lax.axis_index("seq")
        value = k_pre[...]
        turned = rotate(back[:, :size], cos[...], -sin[...])
        key_grad, gain = rms_back(value, rms_scale(value), g_key[5:6, :], turned)
        key_gain[...] = gain
        key_grad = key_grad.astype(BF)
        value_grad = back[:, size:].astype(BF)
        at = 2 * per
        total = part[...] + inner_cols(key_grad, full[:, at : at + size])
        total = total + inner_cols(value_grad, full[:, at + size :])
        value = x[...].astype(F32)
        grad, gain = rms_back(value, rms_scale(value), g_in[0:1, :], total)
        input_grad[...] = mid[...] + grad
        in_gain[...] = gain
        own[:, :width] = hid[...]
        send[:, :width] = hid[...]
        own[:, width : width + per] = q_mine[...]
        send[:, width : width + per] = q_other[...]
        own[:, width + per :] = jnp.where(core == 0, key_grad, value_grad)
        send[:, width + per :] = jnp.where(core == 0, value_grad, key_grad)

    outs = [
        shape((rows, width), F32),
        shape((rows, cols), BF),
        shape((rows, cols), BF),
        shape((1, width), F32),
        shape((1, size), F32),
    ]
    args = [kv_back, key_pre, norm_key, cosine, sine, kv_full, hidden_part, inputs, norm_in]
    args += [middle_grad, hidden, query_mine, query_other]
    flops = 4 * rows * width * size
    far = (1, 3, 4, 5, 6, 7, 9, 10, 11, 12)
    return kernel_call(body, outs, args, flops, far=far, back=(0, 1, 2), room=24)


def late_grads(own, got, gains, width):
    rows, cols = own.shape
    out_cols = cols - width
    shard = width // 4

    def body(a, b, extra, *refs):
        outs, total = refs[:3], refs[3]
        place = lax.axis_index("fsdp")
        total[...] = inner_rows(a[:, :width], a[:, width:]) + inner_rows(b[:, :width], b[:, width:])
        core = lax.axis_index("seq")
        for order, out in enumerate((outs[0], outs[1], outs[2].at[0], outs[2].at[1])):
            flip = order if order in (0, 3) else jnp.where(core == 0, order, 3 - order)
            out[:shard, :] = total[rows_at((place ^ flip) * shard, shard, 16), :].astype(BF)
            out[shard:, :] = extra[place ^ flip]

    block = (shard + gains.shape[1], out_cols)
    outs = [shape(block, BF), shape(block, BF), shape((2, *block), BF)]
    flops = 4 * rows * width * out_cols
    scratch = [pltpu.VMEM((width, out_cols), F32)]
    return kernel_call(
        body, outs, [own, got, gains], flops, scratch, far=(0, 1), back=(0, 1, 2)
    )


def finish(gu_sum, gu_other, rest_sum, rest_other, unit, half):
    width = gu_sum.shape[0]

    def body(gu_a, gu_b, rest_a, rest_b, gate, up, down, out):
        core = lax.axis_index("seq")
        low, high = by_core(core, gu_a[...], gu_b[...])
        gate[:, :unit] = low[:, :unit].astype(F32)
        gate[:, unit:] = high[:, :unit].astype(F32)
        up[:, :unit] = low[:, unit:].astype(F32)
        up[:, unit:] = high[:, unit:].astype(F32)
        low, high = by_core(core, rest_a[...], rest_b[...])
        down[:unit, :] = low[:, :unit].T.astype(F32)
        down[unit:, :] = high[:, :unit].T.astype(F32)
        out[:half, :] = low[:, unit:].T.astype(F32)
        out[half:, :] = high[:, unit:].T.astype(F32)

    outs = [shape((width, 2 * unit), F32)] * 2
    outs += [shape((2 * unit, width), F32), shape((2 * half, width), F32)]
    args = [gu_sum, gu_other, rest_sum, rest_other]
    return kernel_call(body, outs, args, 0, back=(0, 1, 2, 3), room=24)


def pick_half(value, which, axis):
    size = value.shape[axis] // 2
    return lax.dynamic_slice_in_dim(value, which * size, size, axis)


def join_cols(mine, other, core):
    return jnp.where(
        core == 0, jnp.concatenate([mine, other], 1), jnp.concatenate([other, mine], 1)
    ).astype(F32)


def after(value, *others):
    return lax.optimization_barrier((value,) + others)[0]


def on_device(ctx_size):
    def run(
        inputs,
        positions,
        block_ids,
        w_query,
        w_key,
        w_value,
        w_out,
        w_gate,
        w_up,
        w_down,
        gain_in,
        gain_query,
        gain_key,
        gain_attn,
        gain_pre,
        gain_post,
        cotangent,
    ):
        core = lax.axis_index("seq")
        fsdp = lax.axis_index("fsdp")
        seq_rows, model_width = inputs.shape[1:]
        head_size = gain_query.shape[0] * 4
        half_rows = seq_rows // 2
        score_scale = head_size ** (-0.5)
        inputs, cotangent = inputs[0], cotangent[0]

        gains = [gain_in, gain_attn, gain_pre, gain_post, gain_query, gain_key]
        gain_sizes = [member.shape[0] for member in gains]
        shard_rows = w_key.shape[0]
        packed, packed_other = pack(w_query, w_key, w_value, gains)
        first = [packed] + [swap(packed, "fsdp", flip, 4) for flip in (1, 2, 3)]
        first_other = [packed_other] + [swap_pair(block) for block in first[1:]]
        (ffn_mine, ffn_other), unit = pack_ffn(w_gate, w_up, w_down, w_out)
        sent = after(ffn_mine, *first[1:])
        ffn_one = swap(sent, "fsdp", 1, 4)
        ffn_two = swap(sent, "fsdp", 2, 4)

        cosine, sine = tables(positions[0], head_size)
        hidden, key_pre, packed_kv, query_pre, queries, qkv_full, wide_gains, narrow_gains = project(
            inputs, first, first_other, head_size, cosine, sine, block_ids
        )
        if ctx_size == 4:
            kv_one, kv_two = swap(packed_kv, "ctx", 1, 4), swap(packed_kv, "ctx", 3, 4)
            sent = jnp.where(core == 0, kv_one, kv_two)
            ffn_one, ffn_two, sent = lax.optimization_barrier((ffn_one, ffn_two, sent))
            kv_blocks = [packed_kv, kv_one, kv_two, swap_split(sent, "ctx", 4, 3, 1)]
        else:
            kv_all = lax.all_gather(packed_kv, "ctx", axis=0)
        if ctx_size == 4:
            context, logsum = attend_kernel(queries, kv_blocks, score_scale)
        else:
            offsets = jnp.arange(half_rows, dtype=jnp.int32)
            block_all = kv_all[:, seq_rows : seq_rows + 2, 0].astype(jnp.int32)
            key_order = (block_all[:, :, None] * half_rows + offsets).reshape(-1)
            query_order = (block_ids[0][:, None] * half_rows + offsets).reshape(-1)
            key_all = kv_all[:, :seq_rows, :head_size].reshape(-1, head_size)
            value_all = kv_all[:, :seq_rows, head_size:].reshape(-1, head_size)
            by_row = queries.transpose(1, 0, 2)
            seq_out, logsum = attend_forward(
                by_row, key_all, value_all, query_order, key_order, score_scale
            )
            context = seq_out.astype(BF).transpose(1, 0, 2)

        ffn_opposite = swap_split(jnp.where(core == 0, ffn_one, ffn_two), "fsdp", 4, 2, 1)
        ffn_blocks = [ffn_mine, ffn_one, ffn_two, after(ffn_opposite, context)]
        ffn_blocks += [ffn_other] + [swap_pair(block) for block in ffn_blocks[1:]]

        (result, middle_grad, own, send, context_grad, gain_grads), offs = feed_forward(
            inputs,
            cotangent,
            context,
            ffn_blocks,
            unit,
            wide_gains,
        )

        parts = ffn_weight_grads(own, swap_pair(send), offs, unit, head_size // 2)
        order = Order()
        ffn_steps = reduce_steps(parts, ctx_size, (2 * unit,), order)
        next(ffn_steps)
        context_grad = after(context_grad, parts[0])

        if ctx_size == 4:
            *kv_parts, hidden_part, back_mine, back_other, grad_query = attend_back_kernel(
                queries,
                kv_blocks,
                logsum,
                context_grad,
                score_scale,
                query_pre,
                narrow_gains,
                cosine,
                sine,
                qkv_full,
            )
            kv_steps = scatter4(kv_parts, "ctx", 4, 1, 3, order, True)
            next(kv_steps)
        else:
            query_grad, key_grad, value_grad = attend_backward(
                by_row,
                key_all,
                value_all,
                query_order,
                key_order,
                score_scale,
                logsum,
                context_grad.transpose(1, 0, 2),
            )
            query_grad = query_grad.transpose(1, 0, 2)
            kv_grad = jnp.concatenate([key_grad, value_grad], 1).astype(BF)
            hidden_part, back_mine, back_other, grad_query = query_back(
                query_grad, query_pre, narrow_gains, cosine, sine, qkv_full
            )
            kv_back = lax.psum_scatter(kv_grad, "ctx", scatter_dimension=0, tiled=True).astype(F32)
        if ctx_size == 4:
            next(kv_steps)
        next(ffn_steps)
        if ctx_size == 4:
            kv_back = next(kv_steps)
        kv_back = order.wait(kv_back)
        input_grad, own, send, grad_in, grad_key = input_back(
            kv_back,
            key_pre,
            narrow_gains,
            cosine,
            sine,
            qkv_full,
            hidden_part,
            inputs,
            wide_gains,
            middle_grad,
            hidden,
            back_mine,
            back_other,
        )
        gain_list = (grad_in, gain_grads[0], gain_grads[1], gain_grads[2], grad_query, grad_key)
        gain_rows = jnp.concatenate([member.reshape(4, 1, -1) for member in gain_list], 2)
        width = own.shape[1] - model_width
        gain_count = -(-gain_rows.shape[2] // width)
        gain_rows = jnp.pad(gain_rows, ((0, 0), (0, 0), (0, gain_count * width - gain_rows.shape[2])))
        gain_rows = gain_rows.reshape(4, gain_count, width).astype(BF)
        gain_rows = jnp.pad(gain_rows, ((0, 0), (0, 32 - gain_count), (0, 0)))
        late_parts = late_grads(own, swap_pair(send), gain_rows, model_width)
        late_steps = reduce_steps(late_parts, ctx_size, (), order)
        for _ in range(4 if ctx_size == 4 else 2):
            next(late_steps)
            if ctx_size == 4:
                next(ffn_steps)
        next(late_steps)
        (late_sum,), (late_other,) = next(late_steps)
        query_cols = width - head_size
        total_query = join_cols(
            late_sum[:shard_rows, :query_cols], late_other[:shard_rows, :query_cols], core
        )
        total_key = jnp.where(core == 0, late_sum, late_other)[:shard_rows, query_cols:].astype(F32)
        total_value = jnp.where(core == 0, late_other, late_sum)[:shard_rows, query_cols:].astype(F32)
        next(ffn_steps)
        (gu_sum, rest_sum), (gu_other, rest_other) = next(ffn_steps)
        total_gate, total_up, total_down, total_out = finish(
            gu_sum, gu_other, rest_sum, rest_other, unit, head_size // 2
        )
        gain_at = slice(shard_rows, shard_rows + gain_count)
        gain_total = (late_sum[gain_at].astype(F32) + late_other[gain_at].astype(F32)).reshape(-1)
        outs = []
        start = 0
        for size in gain_sizes:
            outs.append(gain_total[start : start + size])
            start += size
        g_in, g_attn, g_pre, g_post, g_query, g_key = outs
        return (
            result[None],
            input_grad[None],
            total_query,
            total_key,
            total_value,
            total_out,
            total_gate,
            total_up,
            total_down,
            g_in,
            g_query,
            g_key,
            g_attn,
            g_pre,
            g_post,
        )

    return run


def solution(mesh):
    rows = P(("seq", "fsdp"), "ctx")
    wide = P(("seq", "fsdp"), "ctx", None)
    first = P("fsdp", None)
    second = P(None, "fsdp")
    flat = P("fsdp")
    in_specs = (wide, rows, rows, first, first, first, first, second, second, first)
    in_specs += (flat,) * 6 + (wide,)
    out_specs = (wide, wide, first, first, first, first, second, second, first) + (flat,) * 6
    return jax.shard_map(
        on_device(mesh.shape["ctx"]),
        mesh=mesh,
        in_specs=in_specs,
        out_specs=out_specs,
        check_vma=False,
    )
```
